256 devices in a mesh: gx: 16 (over y, z_hi), gy: 16 (over x, z_lo, core).
Axes of the slice: x: 4, y: 4, z: 8 (z_hi: 4, z_lo: 2; z = z_hi * 2 + z_lo), core: 2. Of those that a mesh axis runs over, the one named last changes fastest.
Arguments:
- signal: bfloat16 [131072, 384], P(('gx', 'gy')), may hold values from -6 to 6
- w_up: bfloat16 [768, 1536], replicated, may hold values from -0.21875 to 0.21875
- w_down: bfloat16 [768, 1536], replicated, may hold values from -0.15625 to 0.15625
- cotangent: bfloat16 [131072, 384], P(('gx', 'gy')), may hold values from -0.016479492 to 0.016479492
Outputs:
- mixed_out: bfloat16 [131072, 384], P(('gx', 'gy'))
- grad_up: float32 [768, 1536], P('gx', 'gy')
- grad_down: float32 [768, 1536], P('gx', 'gy')
The draws below stay inside these ranges and needn't reach their ends.
All inputs are finite; a program needn't handle non-finite values.
Results may differ from the reference program's by a relative error of at most 0.023.
Values may be sent and summed in bfloat16 or wider, within the bound.
A program may use at most 128 MiB of HBM per device.

```python
import math
import jax
import jax.numpy as jnp
from jax import lax

D = 384
FF = 1536
POS_DEV = 512
D2 = 768
POSITIONS = 131072
N_GY = 16


def block_levels(own_key, extent, pieces, least, largest):
    level = 1.0
    for axis_at, parts in pieces:
        heights = jax.random.uniform(jax.random.fold_in(jax.random.fold_in(own_key, 6), axis_at), (parts,), jnp.float32, least / len(pieces), largest / len(pieces))
        level = level * jnp.repeat(jnp.exp(heights), extent[axis_at] // parts).reshape((-1,) + (1,) * (len(extent) - 1 - axis_at))
    return level


def normal_values(own_key, shape, scale, bound, shards=(), dtype=jnp.bfloat16):
    values = scale * jax.random.normal(own_key, shape, jnp.float32)
    if shards:
        values = values * block_levels(own_key, shape, shards, -0.22, 0.18)
    return jnp.clip(values, -bound, bound).astype(dtype)


def setup_inputs(seed: int = 0) -> dict:
    arg_keys = jax.random.split(jax.random.key(seed), 5)
    return {
        "signal": normal_values(arg_keys[0], (POSITIONS, D), 1.0, 6.0, ((0, 256),)),
        "w_up": normal_values(arg_keys[1], (D2, FF), D2 ** -0.5, 0.21875),
        "w_down": normal_values(arg_keys[2], (D2, FF), FF ** -0.5, 0.15625),
        "cotangent": normal_values(arg_keys[3], (POSITIONS, D), (2 * POSITIONS ** -0.5), 0.016479492, ((0, 256),)),
    }


def normalize(pair):
    values = pair.astype(jnp.float32)
    centre = lax.optimization_barrier(jnp.mean(values, axis=-1, keepdims=True))
    shifted = values - centre
    spread = lax.optimization_barrier(jnp.mean(shifted * shifted, axis=-1, keepdims=True))
    factor = lax.rsqrt(spread + 1e-05)
    return (shifted * factor, factor)

def gelu_value(pre):
    return 0.5 * pre * (1.0 + lax.erf(pre * (1.0 / math.sqrt(2.0))))

def gelu_slope(pre):
    return 0.5 * (1.0 + lax.erf(pre * (1.0 / math.sqrt(2.0)))) + pre * jnp.exp(-0.5 * pre * pre) * (1.0 / math.sqrt(2.0 * math.pi))

def switch_forward(pair, w_up, w_down):
    normed, factor = normalize(pair)
    normed_bf = normed.astype(jnp.bfloat16)
    pre = jnp.dot(normed_bf, w_up, preferred_element_type=jnp.float32)
    hidden = gelu_value(pre).astype(jnp.bfloat16)
    mixed = pair.astype(jnp.float32) + jnp.dot(hidden, w_down.T, preferred_element_type=jnp.float32)
    return (mixed.astype(jnp.bfloat16), pre)

def switch_backward(pair, pre, pair_grad, w_up, w_down, need_input):
    normed, factor = normalize(pair)
    normed_bf = normed.astype(jnp.bfloat16)
    hidden = gelu_value(pre).astype(jnp.bfloat16)
    d_hidden = jnp.dot(pair_grad, w_down, preferred_element_type=jnp.float32)
    grad_down = jnp.dot(pair_grad.T, hidden, preferred_element_type=jnp.float32)
    d_pre = (d_hidden * gelu_slope(pre)).astype(jnp.bfloat16)
    grad_up = jnp.dot(normed_bf.T, d_pre, preferred_element_type=jnp.float32)
    d_input = None
    if need_input:
        d_norm = jnp.dot(d_pre, w_up.T, preferred_element_type=jnp.float32)
        d_pair = factor * (d_norm - lax.optimization_barrier(jnp.mean(d_norm, axis=-1, keepdims=True)) - normed * lax.optimization_barrier(jnp.mean(d_norm * normed, axis=-1, keepdims=True)))
        d_input = (pair_grad.astype(jnp.float32) + d_pair).astype(jnp.bfloat16)
    return (grad_up, grad_down, d_input)

def to_pairs(state, dist):
    width = state.shape[1]
    blocks = state.reshape(-1, 2, dist, width)
    return jnp.concatenate([blocks[:, 0], blocks[:, 1]], axis=-1).reshape(-1, 2 * width)

def from_pairs(pairs, dist, width):
    blocks = pairs.reshape(-1, dist, 2 * width)
    return jnp.stack([blocks[..., :width], blocks[..., width:]], axis=1).reshape(-1, width)

def reference(signal, w_up, w_down, cotangent):
    width = signal.shape[1]
    dists = [POSITIONS // 2, POS_DEV * N_GY, POS_DEV * N_GY // 2, POS_DEV]
    state = signal
    stored = []
    for dist in dists:
        pair = to_pairs(state, dist)
        mixed, pre = switch_forward(pair, w_up, w_down)
        stored.append((pair, pre))
        state = from_pairs(mixed, dist, width)
    mixed_out = state
    grad = cotangent
    total_up = jnp.zeros(w_up.shape, jnp.float32)
    total_down = jnp.zeros(w_down.shape, jnp.float32)
    for section in range(3, -1, -1):
        pair, pre = stored[section]
        pair_grad = to_pairs(grad, dists[section])
        part_up, part_down, d_input = switch_backward(pair, pre, pair_grad, w_up, w_down, section > 0)
        total_up = total_up + part_up
        total_down = total_down + part_down
        if section > 0:
            grad = from_pairs(d_input, dists[section], width)
    return (mixed_out, total_up, total_down)
```

```python
import math

import jax
import jax.numpy as jnp
from jax import lax
from jax.experimental import pallas as pl
from jax.experimental.pallas import tpu as pltpu
from jax.sharding import PartitionSpec as P

MESH = pl.DeviceIdType.MESH
BF = jnp.bfloat16
F32 = jnp.float32
D = 384
D2 = 768
FF = 1536
CH = 32
ROWS = 256
TILE = 256


def dot_nn(left, right):
    return lax.dot_general(left, right, (((1,), (0,)), ((), ())), preferred_element_type=F32)


def dot_nt(left, right):
    return lax.dot_general(left, right, (((1,), (1,)), ((), ())), preferred_element_type=F32)


def kernel(
    sig, cot, wu_hbm, wd_hbm, mixed, gout,
    xs, gs, nbv, gpv, nf, rs, slope, wu, wd, acc, lk, rk, m4, ay, bx, fz, ft,
    sa1, ra1, sa2, ra2, sx1, rx1, sx2, rx2, sb1, rb1, sb2, rb2, sy1, ry1, sy2, ry2, zr, pt, tt,
    sig_s, sig_r, cot_s, cot_r, mix_s, mix_r, loc, lk_s, lk_r, rk_s, rk_r, red_s, red_r,
):
    gx = lax.axis_index("gx")
    gy = lax.axis_index("gy")
    y, zh = gx // 4, gx % 4
    x, zl, c = gy // 4, (gy // 2) % 2, gy % 2
    z = zh * 2 + zl
    ba, bb, bc = y // 2, zh % 2, x // 2
    me = ba * 8 + bb * 4 + bc * 2 + c

    def at(xx, yy, zz, cc):
        return {"gx": yy * 4 + zz // 2, "gy": xx * 4 + (zz % 2) * 2 + cc}

    yp, ym, y2 = (y + 1) % 4, (y + 3) % 4, (y + 2) % 4
    xp, xm = (x + 1) % 4, (x + 3) % 4
    ydev = (at(x, yp, z, c), at(x, ym, z, c))
    xdev = (at(xp, y, z, c), at(xm, y, z, c))
    zdev = [at(x, y, (z + d) % 8, c) for d in range(1, 8)]
    other = at(x, y, z, 1 - c)
    group = []
    for r in range(1, 16):
        ra, rb, rc, rd = r // 8, (r // 4) % 2, (r // 2) % 2, r % 2
        yy = y + ra * (2 - 4 * ba)
        zz = z + rb * (2 - 4 * bb)
        xx = x + rc * (2 - 4 * bc)
        cc = c + rd * (1 - 2 * c)
        target = (yy // 2) * 8 + ((zz // 2) % 2) * 4 + (xx // 2) * 2 + cc
        group.append((r, at(xx, yy, zz, cc), target))

    load_wu = pltpu.make_async_copy(wu_hbm, wu, loc.at[0])
    load_wd = pltpu.make_async_copy(wd_hbm, wd, loc.at[1])
    load_wu.start()
    load_wd.start()
    own_rows = pl.ds(pl.multiple_of(me * CH, CH), CH)
    own_sig = pltpu.make_async_copy(sig.at[own_rows], xs.at[me], loc.at[2])
    own_cot = pltpu.make_async_copy(cot.at[own_rows], gs.at[me], loc.at[3])
    own_sig.start()
    own_cot.start()

    barrier = pltpu.get_barrier_semaphore()
    peers = [dev for _, dev, _ in group] + zdev + list(ydev) + list(xdev)
    for dev in peers:
        pl.semaphore_signal(barrier, inc=1, device_id=dev, device_id_type=MESH)
    pl.semaphore_wait(barrier, len(peers))

    def remote(src, dst, send, recv, dev):
        return pltpu.make_async_remote_copy(
            src_ref=src, dst_ref=dst, send_sem=send, recv_sem=recv, device_id=dev, device_id_type=MESH
        )

    sig_copies, cot_copies = [], []
    for r, dev, target in reversed(group):
        rows = pl.ds(pl.multiple_of(target * CH, CH), CH)
        sig_copies.append(remote(sig.at[rows], xs.at[me], sig_s.at[r], sig_r.at[r], dev))
        cot_copies.append(remote(cot.at[rows], gs.at[me], cot_s.at[r], cot_r.at[r], dev))
    for copy in sig_copies:
        copy.start()
    for copy in cot_copies:
        copy.start()
    load_wu.wait()
    load_wd.wait()
    own_sig.wait()
    for copy in sig_copies:
        copy.wait()

    def low_high(k, i):
        stride = 8 >> k
        low = (i // stride) * 2 * stride + i % stride
        return low, low + stride

    def send_left(k):
        cols = pl.ds(k * ROWS, ROWS)
        into = pl.ds(4 * ROWS + k * ROWS, ROWS)
        return remote(lk.at[1 - c, :, cols], lk.at[1 - c, :, into], lk_s.at[k], lk_r.at[k], other)

    def send_right(k):
        cols = pl.ds(k * ROWS, ROWS)
        into = pl.ds(4 * ROWS + k * ROWS, ROWS)
        return remote(rk.at[1 - c, cols], rk.at[1 - c, into], rk_s.at[k], rk_r.at[k], other)

    for k in range(4):
        for i in range(8):
            low, high = low_high(k, i)
            rows = pl.ds(i * CH, CH)
            pair = jnp.concatenate([xs[low], xs[high]], axis=1).astype(F32)
            centre = jnp.mean(pair, axis=-1, keepdims=True)
            shifted = pair - centre
            spread = jnp.mean(shifted * shifted, axis=-1, keepdims=True)
            factor = lax.rsqrt(spread + 1e-05)
            normed = shifted * factor
            nf[k, rows] = normed
            rs[k, rows] = factor
            nbv[rows] = normed.astype(BF)
        lk[0, :, k * ROWS : (k + 1) * ROWS] = nbv[...].T

        @pl.when(c == 1)
        def _():
            send_left(k).start()

        for j in range(FF // TILE):
            cols = slice(j * TILE, (j + 1) * TILE)
            pre = dot_nn(nbv[...], wu[:, cols])
            half = 0.5 * (1.0 + lax.erf(pre * (1.0 / math.sqrt(2.0))))
            rk[1, k * ROWS : (k + 1) * ROWS, cols] = (pre * half).astype(BF)
            slope[k, :, cols] = half + pre * jnp.exp(-0.5 * pre * pre) * (1.0 / math.sqrt(2.0 * math.pi))

        @pl.when(c == 0)
        def _():
            send_right(k).start()

        for j in range(D2 // TILE):
            cols = slice(j * TILE, (j + 1) * TILE)
            acc[:, cols] = dot_nt(rk[1, k * ROWS : (k + 1) * ROWS], wd[cols])
        for i in range(8):
            low, high = low_high(k, i)
            rows = pl.ds(i * CH, CH)
            xs[low] = (xs[low].astype(F32) + acc[rows, :D]).astype(BF)
            xs[high] = (xs[high].astype(F32) + acc[rows, D:]).astype(BF)

    mix_copies = []
    for r, dev, target in group:
        mix_copies.append(remote(xs.at[target], mixed.at[own_rows], mix_s.at[r], mix_r.at[r], dev))
    own_mix = pltpu.make_async_copy(xs.at[me], mixed.at[own_rows], loc.at[2])
    own_mix.start()
    for copy in mix_copies:
        copy.start()

    own_cot.wait()
    for copy in cot_copies:
        copy.wait()

    for k in (3, 2, 1, 0):
        for i in range(8):
            low, high = low_high(k, i)
            rows = pl.ds(i * CH, CH)
            gpv[rows, :D] = gs[low]
            gpv[rows, D:] = gs[high]
        lk[1, :, k * ROWS : (k + 1) * ROWS] = gpv[...].T

        @pl.when(c == 0)
        def _():
            send_left(k).start()

        for j in range(FF // TILE):
            cols = slice(j * TILE, (j + 1) * TILE)
            d_hidden = dot_nn(gpv[...], wd[:, cols])
            rk[0, k * ROWS : (k + 1) * ROWS, cols] = (d_hidden * slope[k, :, cols]).astype(BF)

        @pl.when(c == 1)
        def _():
            send_right(k).start()

        if k > 0:
            for j in range(D2 // TILE):
                cols = slice(j * TILE, (j + 1) * TILE)
                acc[:, cols] = dot_nt(rk[0, k * ROWS : (k + 1) * ROWS], wu[cols])
            for i in range(8):
                low, high = low_high(k, i)
                rows = pl.ds(i * CH, CH)
                d_norm = acc[rows]
                normed = nf[k, rows]
                first = jnp.mean(d_norm, axis=-1, keepdims=True)
                second = jnp.mean(d_norm * normed, axis=-1, keepdims=True)
                d_pair = rs[k, rows] * (d_norm - first - normed * second)
                gs[low] = (gs[low].astype(F32) + d_pair[:, :D]).astype(BF)
                gs[high] = (gs[high].astype(F32) + d_pair[:, D:]).astype(BF)

    for k in range(4):
        send_left(k).wait()
        send_right(k).wait()

    count = [0]

    def link(src, dst, dev):
        n = count[0]
        count[0] += 1
        return remote(src, dst, red_s.at[n], red_r.at[n], dev)

    def mrow(group_y, half):
        return pl.ds(pl.multiple_of(group_y * 192 + half * 96, 48), 96)

    def hrow(group_y, part):
        return pl.ds(pl.multiple_of(group_y * 192 + part * 48, 48), 48)

    a1 = [[link(sa1.at[i, d], ra1.at[i, d], ydev[d]) for d in range(2)] for i in range(4)]
    a2 = [[link(sa2.at[i, d], ra2.at[i, d], ydev[d]) for d in range(2)] for i in range(4)]
    x1 = [link(sx1.at[d], rx1.at[d], xdev[d]) for d in range(2)]
    x2 = [link(sx2.at[d], rx2.at[d], xdev[d]) for d in range(2)]
    b1 = [link(sb1.at[d], rb1.at[d], xdev[d]) for d in range(2)]
    b2 = [link(sb2.at[d], rb2.at[d], xdev[d]) for d in range(2)]
    y1c = [link(sy1.at[d], ry1.at[d], ydev[d]) for d in range(2)]
    y2c = [link(sy2.at[d], ry2.at[d], ydev[d]) for d in range(2)]

    def unit(i):
        xt = (x + (2, 1, 3, 0)[i]) % 4
        cols = pl.ds(pl.multiple_of(xt * 384, 128), 384)

        def body(t, carry):
            rows = pl.ds(pl.multiple_of(t * 256, 256), 256)
            m4[i, rows] = dot_nn(lk[c, rows], rk[c, :, cols])
            return carry

        lax.fori_loop(0, 3, body, 0)

    def a_first(i):
        for d in range(2):
            sa1[i, d] = m4[i, hrow(y2, d)].astype(BF)
            a1[i][d].start()

    def a_second(i):
        for d, target in enumerate((yp, ym)):
            a1[i][d].wait()
            lo, hi = m4[i, hrow(target, 0)], m4[i, hrow(target, 1)]
            if d == 0:
                lo = lo + ra1[i, d].astype(F32)
            else:
                hi = hi + ra1[i, d].astype(F32)
            sa2[i, d, :48] = lo.astype(BF)
            sa2[i, d, 48:] = hi.astype(BF)
            a2[i][d].start()

    def a_final(i):
        for d in range(2):
            a2[i][d].wait()
        ay[i] = m4[i, mrow(y, 0)] + ra2[i, 0].astype(F32) + ra2[i, 1].astype(F32)

    def b_first():
        for d in range(2):
            for g in range(2):
                sb1[d, g] = m4[0, mrow(2 * d + g, 1)].astype(BF)
            b1[d].start()

    def b_second(d):
        b1[d].wait()
        for g in range(4):
            value = m4[1 + d, mrow(g, 1)]
            if g // 2 == d:
                value = value + rb1[d, g % 2].astype(F32)
            sb2[d, g] = value.astype(BF)
        b2[d].start()

    unit(0)
    a_first(0)
    b_first()
    unit(1)
    a_first(1)
    b_second(0)
    a_second(0)
    unit(2)
    a_first(2)
    b_second(1)
    a_second(1)
    unit(3)
    a_first(3)
    a_second(2)
    a_final(0)
    for d in range(2):
        sx1[d] = ay[0, d * 48 : (d + 1) * 48].astype(BF)
        x1[d].start()
    a_second(3)
    for d in range(2):
        b2[d].wait()
    for g in range(4):
        bx[g] = m4[3, mrow(g, 1)] + rb2[0, g].astype(F32) + rb2[1, g].astype(F32)
    for d in range(2):
        sy1[d] = bx[y2, d * 48 : (d + 1) * 48].astype(BF)
        y1c[d].start()
    for d in range(2):
        a_final(1 + d)
        x1[d].wait()
        rows = slice(d * 48, (d + 1) * 48)
        ay[1 + d, rows] = ay[1 + d, rows] + rx1[d].astype(F32)
        sx2[d] = ay[1 + d].astype(BF)
        x2[d].start()
    for d, target in enumerate((yp, ym)):
        y1c[d].wait()
        rows = slice(d * 48, (d + 1) * 48)
        bx[target, rows] = bx[target, rows] + ry1[d].astype(F32)
        sy2[d] = bx[target].astype(BF)
        y2c[d].start()
    a_final(3)
    for d in range(2):
        x2[d].wait()
    ft[:96] = ay[3] + rx2[0].astype(F32) + rx2[1].astype(F32)
    for d in range(2):
        y2c[d].wait()
    ft[96:] = bx[y] + ry2[0].astype(F32) + ry2[1].astype(F32)
    fz[...] = ft[...].astype(BF)

    z_copies = []
    for d in range(1, 8):
        zd = (z + d) % 8
        rows = pl.ds(pl.multiple_of((zd // 2) * 48, 48), 48)
        cols = pl.ds(pl.multiple_of((zd % 2) * 128, 128), 256)
        z_copies.append(link(fz.at[rows, cols], zr.at[d - 1], zdev[d - 1]))
    for copy in z_copies:
        copy.start()
    rows = pl.ds(pl.multiple_of(zh * 48, 48), 48)
    cols = pl.ds(pl.multiple_of(zl * 128, 128), 256)
    total = ft[rows, cols]
    for d in range(7):
        z_copies[d].wait()
        total = total + zr[d].astype(F32)
    tt[...] = total
    last = link(tt, pt, other)
    last.start()
    gout[c] = total
    last.wait()
    gout[1 - c] = pt[...]

    own_mix.wait()
    for copy in mix_copies:
        copy.wait()


def local(signal, w_up, w_down, cotangent):
    vm = pltpu.VMEM
    dma = pltpu.SemaphoreType.DMA
    anyspec = pl.BlockSpec(memory_space=pl.ANY)
    mixed, grads = pl.pallas_call(
        kernel,
        out_shape=(
            jax.ShapeDtypeStruct((512, D), BF),
            jax.ShapeDtypeStruct((2, 48, 256), F32),
        ),
        in_specs=[anyspec] * 4,
        out_specs=(anyspec, pl.BlockSpec(memory_space=pltpu.VMEM)),
        scratch_shapes=[
            vm((16, CH, D), BF), vm((16, CH, D), BF), vm((ROWS, D2), BF), vm((ROWS, D2), BF),
            vm((4, ROWS, D2), F32), vm((4, ROWS, 1), F32), vm((4, ROWS, FF), F32),
            vm((D2, FF), BF), vm((D2, FF), BF), vm((ROWS, D2), F32),
            vm((2, D2, 8 * ROWS), BF), vm((2, 8 * ROWS, FF), BF),
            vm((4, D2, D), F32), vm((4, 96, D), F32), vm((4, 96, D), F32),
            vm((192, D), BF), vm((192, D), F32),
            vm((4, 2, 48, D), BF), vm((4, 2, 48, D), BF),
            vm((4, 2, 96, D), BF), vm((4, 2, 96, D), BF),
            vm((2, 48, D), BF), vm((2, 48, D), BF), vm((2, 96, D), BF), vm((2, 96, D), BF),
            vm((2, 2, 96, D), BF), vm((2, 2, 96, D), BF),
            vm((2, 4, 96, D), BF), vm((2, 4, 96, D), BF),
            vm((2, 48, D), BF), vm((2, 48, D), BF), vm((2, 96, D), BF), vm((2, 96, D), BF),
            vm((7, 48, 256), BF), vm((48, 256), F32), vm((48, 256), F32),
            dma((16,)), dma((16,)), dma((16,)), dma((16,)), dma((16,)), dma((16,)),
            dma((4,)), dma((4,)), dma((4,)), dma((4,)), dma((4,)),
            dma((40,)), dma((40,)),
        ],
        compiler_params=pltpu.CompilerParams(
            collective_id=0, has_side_effects=True, vmem_limit_bytes=62 << 20
        ),
    )(signal, cotangent, w_up, w_down)
    gy = lax.axis_index("gy")
    start = (gy // 2) % 2 * 64 + gy % 2 * 96
    blocks = lax.dynamic_slice(grads, (0, 0, start), (2, 48, 96))
    return (mixed, blocks[0], blocks[1])


def solution(mesh):
    return jax.shard_map(
        local,
        mesh=mesh,
        in_specs=(P(("gx", "gy"), None), P(), P(), P(("gx", "gy"), None)),
        out_specs=(P(("gx", "gy"), None), P("gx", "gy"), P("gx", "gy")),
        check_vma=False,
    )
```

```python
import math

import jax
import jax.numpy as jnp
from jax import lax
from jax.experimental import pallas as pl
from jax.experimental.pallas import tpu as pltpu
from jax.sharding import PartitionSpec as P

MESH = pl.DeviceIdType.MESH
BF = jnp.bfloat16
F32 = jnp.float32
D = 384
D2 = 768
FF = 1536
CH = 32
ROWS = 256
TILE = 256


def dot_nn(left, right):
    return lax.dot_general(left, right, (((1,), (0,)), ((), ())), preferred_element_type=F32)


def dot_nt(left, right):
    return lax.dot_general(left, right, (((1,), (1,)), ((), ())), preferred_element_type=F32)


def kernel(
    sig, cot, wu_hbm, wd_hbm, mixed, gout,
    xs, gs, nbv, gpv, nf, rs, slope, prev, wu, wd, acc, lk, rk, m4, ay, bx, fz, ft,
    sa1, ra1, sa2, ra2, sx1, rx1, sx2, rx2, sb1, rb1, sb2, rb2, sy1, ry1, sy2, ry2, zr, pt, tt,
    sig_s, sig_r, cot_s, cot_r, mix_s, mix_r, loc, lk_s, lk_r, rk_s, rk_r, red_s, red_r,
):
    gx = lax.axis_index("gx")
    gy = lax.axis_index("gy")
    y, zh = gx // 4, gx % 4
    x, zl, c = gy // 4, (gy // 2) % 2, gy % 2
    z = zh * 2 + zl
    ba, bb, bc = y // 2, zh % 2, x // 2
    me = ba * 8 + bb * 4 + bc * 2 + c

    def at(xx, yy, zz, cc):
        return {"gx": yy * 4 + zz // 2, "gy": xx * 4 + (zz % 2) * 2 + cc}

    yp, ym, y2 = (y + 1) % 4, (y + 3) % 4, (y + 2) % 4
    xp, xm = (x + 1) % 4, (x + 3) % 4
    ydev = (at(x, yp, z, c), at(x, ym, z, c))
    xdev = (at(xp, y, z, c), at(xm, y, z, c))
    zdev = [at(x, y, (z + d) % 8, c) for d in range(1, 8)]
    other = at(x, y, z, 1 - c)
    group = []
    for r in range(1, 16):
        ra, rb, rc, rd = r // 8, (r // 4) % 2, (r // 2) % 2, r % 2
        yy = y + ra * (2 - 4 * ba)
        zz = z + rb * (2 - 4 * bb)
        xx = x + rc * (2 - 4 * bc)
        cc = c + rd * (1 - 2 * c)
        target = (yy // 2) * 8 + ((zz // 2) % 2) * 4 + (xx // 2) * 2 + cc
        group.append((r, at(xx, yy, zz, cc), target))

    load_wu = pltpu.make_async_copy(wu_hbm, wu, loc.at[0])
    load_wd = pltpu.make_async_copy(wd_hbm, wd, loc.at[1])
    load_wu.start()
    load_wd.start()
    own_rows = pl.ds(pl.multiple_of(me * CH, CH), CH)
    own_sig = pltpu.make_async_copy(sig.at[own_rows], xs.at[me], loc.at[2])
    own_cot = pltpu.make_async_copy(cot.at[own_rows], gs.at[me], loc.at[3])
    own_sig.start()
    own_cot.start()

    barrier = pltpu.get_barrier_semaphore()
    peers = [dev for _, dev, _ in group] + zdev + list(ydev) + list(xdev)
    for dev in peers:
        pl.semaphore_signal(barrier, inc=1, device_id=dev, device_id_type=MESH)
    pl.semaphore_wait(barrier, len(peers))

    def remote(src, dst, send, recv, dev):
        return pltpu.make_async_remote_copy(
            src_ref=src, dst_ref=dst, send_sem=send, recv_sem=recv, device_id=dev, device_id_type=MESH
        )

    sig_copies, cot_copies = [], []
    for r, dev, target in reversed(group):
        rows = pl.ds(pl.multiple_of(target * CH, CH), CH)
        sig_copies.append(remote(sig.at[rows], xs.at[me], sig_s.at[r], sig_r.at[r], dev))
        cot_copies.append(remote(cot.at[rows], gs.at[me], cot_s.at[r], cot_r.at[r], dev))
    for copy in sig_copies:
        copy.start()
    load_wu.wait()
    load_wd.wait()
    own_sig.wait()
    for copy in sig_copies:
        copy.wait()
    for copy in cot_copies:
        copy.start()

    def low_high(k, i):
        stride = 8 >> k
        low = (i // stride) * 2 * stride + i % stride
        return low, low + stride

    def send_left(k):
        cols = pl.ds(k * ROWS, ROWS)
        into = pl.ds(4 * ROWS + k * ROWS, ROWS)
        return remote(lk.at[1 - c, :, cols], lk.at[1 - c, :, into], lk_s.at[k], lk_r.at[k], other)

    def send_right(k):
        cols = pl.ds(k * ROWS, ROWS)
        into = pl.ds(4 * ROWS + k * ROWS, ROWS)
        return remote(rk.at[1 - c, cols], rk.at[1 - c, into], rk_s.at[k], rk_r.at[k], other)

    for k in range(4):
        for i in range(8):
            low, high = low_high(k, i)
            rows = pl.ds(i * CH, CH)
            pair = jnp.concatenate([xs[low], xs[high]], axis=1).astype(F32)
            centre = jnp.mean(pair, axis=-1, keepdims=True)
            shifted = pair - centre
            spread = jnp.mean(shifted * shifted, axis=-1, keepdims=True)
            factor = lax.rsqrt(spread + 1e-05)
            normed = shifted * factor
            nf[k, rows] = normed
            rs[k, rows] = factor
            nbv[rows] = normed.astype(BF)
        mine = slice(k * ROWS, (k + 1) * ROWS)
        for j in range(FF // TILE):
            cols = slice(j * TILE, (j + 1) * TILE)
            pre = dot_nn(nbv[...], wu[:, cols])
            half = 0.5 + 0.5 * lax.erf(pre * (1.0 / math.sqrt(2.0)))
            rk[1, mine, cols] = (pre * half).astype(BF)
            prev[:, cols] = pre
            slope[k, :, cols] = half
            if j % 2 == 1:
                part = slice(j // 2 * TILE, (j // 2 + 1) * TILE)
                lk[0, part, mine] = nbv[:, part].T
        for j in range(D2 // TILE):
            cols = slice(j * TILE, (j + 1) * TILE)
            out = dot_nt(rk[1, mine], wd[cols])
            for i in range(8):
                low, high = low_high(k, i)
                for at_pos, first in ((low, 0), (high, D)):
                    lo, hi = max(first, j * TILE), min(first + D, (j + 1) * TILE)
                    if lo < hi:
                        here = slice(lo - first, hi - first)
                        value = out[i * CH : (i + 1) * CH, lo - j * TILE : hi - j * TILE]
                        xs[at_pos, :, here] = (xs[at_pos, :, here].astype(F32) + value).astype(BF)
            for t in (2 * j, 2 * j + 1):
                cols = slice(t * TILE, (t + 1) * TILE)
                pre = prev[:, cols]
                bell = jnp.exp2(pre * pre * (-0.5 * math.log2(math.e)))
                slope[k, :, cols] = slope[k, :, cols] + pre * (1.0 / math.sqrt(2.0 * math.pi)) * bell

        @pl.when(c == 1)
        def _():
            send_left(k).start()

        @pl.when(c == 0)
        def _():
            send_right(k).start()

    mix_copies = []
    for r, dev, target in group:
        mix_copies.append(remote(xs.at[target], mixed.at[own_rows], mix_s.at[r], mix_r.at[r], dev))
    own_mix = pltpu.make_async_copy(xs.at[me], mixed.at[own_rows], loc.at[2])
    own_mix.start()
    for copy in mix_copies:
        copy.start()

    own_cot.wait()
    for copy in cot_copies:
        copy.wait()

    for k in (3, 2, 1, 0):
        for i in range(8):
            low, high = low_high(k, i)
            rows = pl.ds(i * CH, CH)
            gpv[rows, :D] = gs[low]
            gpv[rows, D:] = gs[high]
        mine = slice(k * ROWS, (k + 1) * ROWS)
        for j in range(FF // TILE):
            cols = slice(j * TILE, (j + 1) * TILE)
            d_hidden = dot_nn(gpv[...], wd[:, cols])
            rk[0, mine, cols] = (d_hidden * slope[k, :, cols]).astype(BF)
            if j < 3:
                part = slice(j * TILE, (j + 1) * TILE)
                lk[1, part, mine] = gpv[:, part].T

        @pl.when(c == 0)
        def _():
            send_left(k).start()

        @pl.when(c == 1)
        def _():
            send_right(k).start()

        if k > 0:
            for j in range(D2 // TILE):
                cols = slice(j * TILE, (j + 1) * TILE)
                acc[:, cols] = dot_nt(rk[0, k * ROWS : (k + 1) * ROWS], wu[cols])
            for i in range(8):
                low, high = low_high(k, i)
                rows = pl.ds(i * CH, CH)
                d_norm = acc[rows]
                normed = nf[k, rows]
                first = jnp.mean(d_norm, axis=-1, keepdims=True)
                second = jnp.mean(d_norm * normed, axis=-1, keepdims=True)
                d_pair = rs[k, rows] * (d_norm - first - normed * second)
                gs[low] = (gs[low].astype(F32) + d_pair[:, :D]).astype(BF)
                gs[high] = (gs[high].astype(F32) + d_pair[:, D:]).astype(BF)

    for k in range(4):
        send_left(k).wait()
        send_right(k).wait()

    count = [0]

    def link(src, dst, dev):
        n = count[0]
        count[0] += 1
        return remote(src, dst, red_s.at[n], red_r.at[n], dev)

    def mrow(group_y, half):
        return pl.ds(pl.multiple_of(group_y * 192 + half * 96, 48), 96)

    def hrow(group_y, part):
        return pl.ds(pl.multiple_of(group_y * 192 + part * 48, 48), 48)

    def span(first, size=48):
        return pl.ds(first * 48, size)

    a1 = [[link(sa1.at[i, d], ra1.at[i, d], ydev[d]) for d in range(2)] for i in range(4)]
    a2 = [
        [[link(sa2.at[i, d, span(h)], ra2.at[i, d, span(h)], ydev[d]) for h in range(2)] for d in range(2)]
        for i in range(4)
    ]
    x1 = [link(sx1.at[d], rx1.at[d], xdev[d]) for d in range(2)]
    x2 = [[link(sx2.at[d, span(h)], rx2.at[d, span(h)], xdev[d]) for h in range(2)] for d in range(2)]
    b1 = [[link(sb1.at[d, g], rb1.at[d, g], xdev[d]) for g in range(2)] for d in range(2)]
    b2 = [[link(sb2.at[d, g], rb2.at[d, g], xdev[d]) for g in range(4)] for d in range(2)]
    y1c = [link(sy1.at[d], ry1.at[d], ydev[d]) for d in range(2)]
    y2c = [[link(sy2.at[d, span(h)], ry2.at[d, span(h)], ydev[d]) for h in range(2)] for d in range(2)]
    near = (yp, ym)

    def unit_cols(i, first, size):
        xt = (x + (2, 1, 3, 0)[i]) % 4
        return pl.ds(pl.multiple_of(xt * 384 + first, 128), size)

    def wide(i):
        def body(t, carry):
            rows = pl.ds(pl.multiple_of(t * 256, 256), 256)
            m4[i, rows, :256] = dot_nn(lk[c, rows], rk[c, :, unit_cols(i, 0, 256)])
            return carry

        lax.fori_loop(0, 3, body, 0)

    def shared(i):
        def body(t, carry):
            rows = pl.ds(pl.multiple_of(t * 256, 256), 256)
            right = jnp.concatenate(
                [rk[c, :, unit_cols(i, 256, 128)], rk[c, :, unit_cols(i + 1, 256, 128)]], axis=1
            )
            out = dot_nn(lk[c, rows], right)
            m4[i, rows, 256:] = out[:, :128]
            m4[i + 1, rows, 256:] = out[:, 128:]
            return carry

        lax.fori_loop(0, 3, body, 0)

    def a_open(i):
        for d in range(2):
            sa1[i, d] = m4[i, hrow(y2, d)].astype(BF)
            a1[i][d].start()
        for d in range(2):
            sa2[i, d, (1 - d) * 48 : (2 - d) * 48] = m4[i, hrow(near[d], 1 - d)].astype(BF)
            a2[i][d][1 - d].start()

    def a_pass(i):
        for d in range(2):
            a1[i][d].wait()
            sa2[i, d, d * 48 : (d + 1) * 48] = (m4[i, hrow(near[d], d)] + ra1[i, d].astype(F32)).astype(BF)
            a2[i][d][d].start()

    def a_final(i):
        for d in range(2):
            a2[i][d][1 - d].wait()
            a2[i][d][d].wait()
        ay[i] = m4[i, mrow(y, 0)] + ra2[i, 0].astype(F32) + ra2[i, 1].astype(F32)

    def b_open():
        for g in range(2):
            for d in range(2):
                sb1[d, g] = m4[0, mrow(2 * d + g, 1)].astype(BF)
                b1[d][g].start()

    def b_free(d):
        for g in (2 - 2 * d, 3 - 2 * d):
            sb2[d, g] = m4[1 + d, mrow(g, 1)].astype(BF)
            b2[d][g].start()

    def b_pass(d):
        for h in range(2):
            g = 2 * d + h
            b1[d][h].wait()
            sb2[d, g] = (m4[1 + d, mrow(g, 1)] + rb1[d, h].astype(F32)).astype(BF)
            b2[d][g].start()

    wide(0)
    shared(0)
    b_open()
    a_open(0)
    wide(1)
    b_free(0)
    a_open(1)
    wide(2)
    a_pass(0)
    shared(2)
    b_free(1)
    a_open(2)
    b_pass(0)
    b_pass(1)
    wide(3)
    a_open(3)
    a_pass(1)
    a_pass(2)
    a_final(0)
    for d in range(2):
        sx1[d] = ay[0, d * 48 : (d + 1) * 48].astype(BF)
        x1[d].start()
    a_pass(3)
    for d in range(2):
        a_final(1 + d)
        free = slice((1 - d) * 48, (2 - d) * 48)
        sx2[d, free] = ay[1 + d, free].astype(BF)
        x2[d][1 - d].start()
    for d in range(2):
        for g in range(4):
            b2[d][g].wait()
    for g in range(4):
        bx[g] = m4[3, mrow(g, 1)] + rb2[0, g].astype(F32) + rb2[1, g].astype(F32)
    for d in range(2):
        sy1[d] = bx[y2, d * 48 : (d + 1) * 48].astype(BF)
        y1c[d].start()
    for d in range(2):
        free = slice((1 - d) * 48, (2 - d) * 48)
        sy2[d, free] = bx[near[d], free].astype(BF)
        y2c[d][1 - d].start()
    for d in range(2):
        x1[d].wait()
        held = slice(d * 48, (d + 1) * 48)
        sx2[d, held] = (ay[1 + d, held] + rx1[d].astype(F32)).astype(BF)
        x2[d][d].start()
    a_final(3)
    for d in range(2):
        y1c[d].wait()
        held = slice(d * 48, (d + 1) * 48)
        sy2[d, held] = (bx[near[d], held] + ry1[d].astype(F32)).astype(BF)
        y2c[d][d].start()

    z_copies = []
    for d in range(1, 8):
        zd = (z + d) % 8
        rows = pl.ds(pl.multiple_of((zd // 2) * 48, 48), 48)
        cols = pl.ds(pl.multiple_of((zd % 2) * 128, 128), 256)
        z_copies.append((zd, link(fz.at[rows, cols], zr.at[d - 1], zdev[d - 1])))

    def z_send(part):
        for zd, copy in z_copies:

            @pl.when(zd // 4 == part)
            def _():
                copy.start()

    for d in range(2):
        x2[d][1 - d].wait()
        x2[d][d].wait()
    ft[:96] = ay[3] + rx2[0].astype(F32) + rx2[1].astype(F32)
    fz[:96] = ft[:96].astype(BF)
    z_send(0)
    for d in range(2):
        y2c[d][1 - d].wait()
        y2c[d][d].wait()
    ft[96:] = bx[y] + ry2[0].astype(F32) + ry2[1].astype(F32)
    fz[96:] = ft[96:].astype(BF)
    z_send(1)
    rows = pl.ds(pl.multiple_of(zh * 48, 48), 48)
    cols = pl.ds(pl.multiple_of(zl * 128, 128), 256)
    total = ft[rows, cols]
    for d in range(7):
        z_copies[d][1].wait()
        total = total + zr[d].astype(F32)
    tt[...] = total
    last = link(tt, pt, other)
    last.start()
    gout[c] = total
    last.wait()
    gout[1 - c] = pt[...]

    own_mix.wait()
    for copy in mix_copies:
        copy.wait()


def finish(mixed, grads, mixed_out, up_out, down_out):
    gy = lax.axis_index("gy")
    start = (gy // 2) % 2 * 64 + gy % 2 * 96
    mixed_out[...] = mixed[...]
    for i, out in enumerate((up_out, down_out)):
        out[...] = pltpu.roll(grads[i], (256 - start) % 256, 1)[:, :96]


def local(signal, w_up, w_down, cotangent):
    vm = pltpu.VMEM
    dma = pltpu.SemaphoreType.DMA
    anyspec = pl.BlockSpec(memory_space=pl.ANY)
    mixed, grads = pl.pallas_call(
        kernel,
        out_shape=(
            jax.ShapeDtypeStruct((512, D), BF),
            jax.ShapeDtypeStruct((2, 48, 256), F32),
        ),
        in_specs=[anyspec] * 4,
        out_specs=(anyspec, pl.BlockSpec(memory_space=pltpu.VMEM)),
        scratch_shapes=[
            vm((16, CH, D), BF), vm((16, CH, D), BF), vm((ROWS, D2), BF), vm((ROWS, D2), BF),
            vm((4, ROWS, D2), F32), vm((4, ROWS, 1), F32), vm((4, ROWS, FF), F32), vm((ROWS, FF), F32),
            vm((D2, FF), BF), vm((D2, FF), BF), vm((ROWS, D2), F32),
            vm((2, D2, 8 * ROWS), BF), vm((2, 8 * ROWS, FF), BF),
            vm((4, D2, D), F32), vm((4, 96, D), F32), vm((4, 96, D), F32),
            vm((192, D), BF), vm((192, D), F32),
            vm((4, 2, 48, D), BF), vm((4, 2, 48, D), BF),
            vm((4, 2, 96, D), BF), vm((4, 2, 96, D), BF),
            vm((2, 48, D), BF), vm((2, 48, D), BF), vm((2, 96, D), BF), vm((2, 96, D), BF),
            vm((2, 2, 96, D), BF), vm((2, 2, 96, D), BF),
            vm((2, 4, 96, D), BF), vm((2, 4, 96, D), BF),
            vm((2, 48, D), BF), vm((2, 48, D), BF), vm((2, 96, D), BF), vm((2, 96, D), BF),
            vm((7, 48, 256), BF), vm((48, 256), F32), vm((48, 256), F32),
            dma((16,)), dma((16,)), dma((16,)), dma((16,)), dma((16,)), dma((16,)),
            dma((4,)), dma((4,)), dma((4,)), dma((4,)), dma((4,)),
            dma((64,)), dma((64,)),
        ],
        compiler_params=pltpu.CompilerParams(
            collective_id=0, has_side_effects=True, vmem_limit_bytes=62 << 20
        ),
    )(signal, cotangent, w_up, w_down)
    return pl.pallas_call(
        finish,
        out_shape=(
            jax.ShapeDtypeStruct((512, D), BF),
            jax.ShapeDtypeStruct((48, 96), F32),
            jax.ShapeDtypeStruct((48, 96), F32),
        ),
        in_specs=[pl.BlockSpec(memory_space=pltpu.VMEM)] * 2,
        out_specs=(pl.BlockSpec(memory_space=pltpu.VMEM),) * 3,
    )(mixed, grads)


def solution(mesh):
    return jax.shard_map(
        local,
        mesh=mesh,
        in_specs=(P(("gx", "gy"), None), P(), P(), P(("gx", "gy"), None)),
        out_specs=(P(("gx", "gy"), None), P("gx", "gy"), P("gx", "gy")),
        check_vma=False,
    )
```

```python
import math

import jax
import jax.numpy as jnp
from jax import lax
from jax.experimental import pallas as pl
from jax.experimental.pallas import tpu as pltpu
from jax.sharding import PartitionSpec as P

MESH = pl.DeviceIdType.MESH
BF = jnp.bfloat16
F32 = jnp.float32
D = 384
D2 = 768
FF = 1536
CH = 32
ROWS = 256
TILE = 256


def dot_nn(left, right):
    return lax.dot_general(left, right, (((1,), (0,)), ((), ())), preferred_element_type=F32)


def dot_nt(left, right):
    return lax.dot_general(left, right, (((1,), (1,)), ((), ())), preferred_element_type=F32)


def kernel(
    sig, cot, wu_hbm, wd_hbm, mixed, gout,
    xs, gs, nbv, gpv, nf, rs, slope, prev, wu, wd, acc, lk, rk, m4, ay, bx, fz, ft,
    sa1, ra1, sa2, ra2, sx1, rx1, sx2, rx2, sb1, rb1, sb2, rb2, sy1, ry1, sy2, ry2, zr, pt, tt,
    sig_s, sig_r, cot_s, cot_r, mix_s, mix_r, loc, lk_s, lk_r, rk_s, rk_r, red_s, red_r,
):
    gx = lax.axis_index("gx")
    gy = lax.axis_index("gy")
    y, zh = gx // 4, gx % 4
    x, zl, c = gy // 4, (gy // 2) % 2, gy % 2
    z = zh * 2 + zl
    ba, bb, bc = y // 2, zh % 2, x // 2
    me = ba * 8 + bb * 4 + bc * 2 + c

    def at(xx, yy, zz, cc):
        return {"gx": yy * 4 + zz // 2, "gy": xx * 4 + (zz % 2) * 2 + cc}

    yp, ym, y2 = (y + 1) % 4, (y + 3) % 4, (y + 2) % 4
    xp, xm = (x + 1) % 4, (x + 3) % 4
    ydev = (at(x, yp, z, c), at(x, ym, z, c))
    xdev = (at(xp, y, z, c), at(xm, y, z, c))
    zdev = [at(x, y, (z + d) % 8, c) for d in range(1, 8)]
    other = at(x, y, z, 1 - c)
    group = []
    for r in range(1, 16):
        ra, rb, rc, rd = r // 8, (r // 4) % 2, (r // 2) % 2, r % 2
        yy = y + ra * (2 - 4 * ba)
        zz = z + rb * (2 - 4 * bb)
        xx = x + rc * (2 - 4 * bc)
        cc = c + rd * (1 - 2 * c)
        target = (yy // 2) * 8 + ((zz // 2) % 2) * 4 + (xx // 2) * 2 + cc
        group.append((r, at(xx, yy, zz, cc), target))

    load_wu = pltpu.make_async_copy(wu_hbm, wu, loc.at[0])
    load_wd = pltpu.make_async_copy(wd_hbm, wd, loc.at[1])
    load_wu.start()
    load_wd.start()
    own_rows = pl.ds(pl.multiple_of(me * CH, CH), CH)
    own_sig = pltpu.make_async_copy(sig.at[own_rows], xs.at[me], loc.at[2])
    own_cot = pltpu.make_async_copy(cot.at[own_rows], gs.at[me], loc.at[3])
    own_sig.start()
    own_cot.start()

    barrier = pltpu.get_barrier_semaphore()
    peers = [dev for _, dev, _ in group] + zdev + list(ydev) + list(xdev)
    for dev in peers:
        pl.semaphore_signal(barrier, inc=1, device_id=dev, device_id_type=MESH)
    pl.semaphore_wait(barrier, len(peers))

    def remote(src, dst, send, recv, dev):
        return pltpu.make_async_remote_copy(
            src_ref=src, dst_ref=dst, send_sem=send, recv_sem=recv, device_id=dev, device_id_type=MESH
        )

    sig_copies, cot_copies = [], []
    for r, dev, target in reversed(group):
        rows = pl.ds(pl.multiple_of(target * CH, CH), CH)
        sig_copies.append(remote(sig.at[rows], xs.at[me], sig_s.at[0], sig_r.at[0], dev))
        cot_copies.append(remote(cot.at[rows], gs.at[me], cot_s.at[0], cot_r.at[0], dev))
    for copy in sig_copies:
        copy.start()
    load_wu.wait()
    load_wd.wait()
    own_sig.wait()
    most = pl.ds(0, 15)
    wide_rows = pl.ds(0, 15 * CH)
    all_sig = remote(sig.at[wide_rows], xs.at[most], sig_s.at[0], sig_r.at[0], other)
    all_cot = remote(cot.at[wide_rows], gs.at[most], cot_s.at[0], cot_r.at[0], other)
    all_mix = remote(xs.at[most], mixed.at[wide_rows], mix_s.at[0], mix_r.at[0], other)
    all_sig.wait_send()
    for copy in cot_copies:
        copy.start()
    all_sig.wait_recv()

    def low_high(k, i):
        stride = 8 >> k
        low = (i // stride) * 2 * stride + i % stride
        return low, low + stride

    def send_left(k):
        cols = pl.ds(k * ROWS, ROWS)
        into = pl.ds(4 * ROWS + k * ROWS, ROWS)
        return remote(lk.at[1 - c, :, cols], lk.at[1 - c, :, into], lk_s.at[k], lk_r.at[k], other)

    def send_right(k):
        cols = pl.ds(k * ROWS, ROWS)
        into = pl.ds(4 * ROWS + k * ROWS, ROWS)
        return remote(rk.at[1 - c, cols], rk.at[1 - c, into], rk_s.at[k], rk_r.at[k], other)

    for k in range(4):
        for i in range(8):
            low, high = low_high(k, i)
            rows = pl.ds(i * CH, CH)
            pair = jnp.concatenate([xs[low], xs[high]], axis=1).astype(F32)
            centre = jnp.mean(pair, axis=-1, keepdims=True)
            shifted = pair - centre
            spread = jnp.mean(shifted * shifted, axis=-1, keepdims=True)
            factor = lax.rsqrt(spread + 1e-05)
            normed = shifted * factor
            nf[k, rows] = normed
            rs[k, rows] = factor
            nbv[rows] = normed.astype(BF)
        mine = slice(k * ROWS, (k + 1) * ROWS)
        for j in range(FF // TILE):
            cols = slice(j * TILE, (j + 1) * TILE)
            pre = dot_nn(nbv[...], wu[:, cols])
            half = 0.5 + 0.5 * lax.erf(pre * (1.0 / math.sqrt(2.0)))
            rk[1, mine, cols] = (pre * half).astype(BF)
            prev[:, cols] = pre
            slope[k, :, cols] = half
            if j % 2 == 1:
                part = slice(j // 2 * TILE, (j // 2 + 1) * TILE)
                lk[0, part, mine] = nbv[:, part].T

        @pl.when(c == 0)
        def _():
            send_right(k).start()

        for j in range(D2 // TILE):
            cols = slice(j * TILE, (j + 1) * TILE)
            out = dot_nt(rk[1, mine], wd[cols])
            for i in range(8):
                low, high = low_high(k, i)
                for at_pos, first in ((low, 0), (high, D)):
                    lo, hi = max(first, j * TILE), min(first + D, (j + 1) * TILE)
                    if lo < hi:
                        here = slice(lo - first, hi - first)
                        value = out[i * CH : (i + 1) * CH, lo - j * TILE : hi - j * TILE]
                        xs[at_pos, :, here] = (xs[at_pos, :, here].astype(F32) + value).astype(BF)
            for t in (2 * j, 2 * j + 1):
                cols = slice(t * TILE, (t + 1) * TILE)
                pre = prev[:, cols]
                bell = jnp.exp2(pre * pre * (-0.5 * math.log2(math.e)))
                slope[k, :, cols] = slope[k, :, cols] + pre * (1.0 / math.sqrt(2.0 * math.pi)) * bell

        @pl.when(c == 1)
        def _():
            send_left(k).start()

    mix_copies = []
    for r, dev, target in group:
        mix_copies.append(remote(xs.at[target], mixed.at[own_rows], mix_s.at[0], mix_r.at[0], dev))
    own_mix = pltpu.make_async_copy(xs.at[me], mixed.at[own_rows], loc.at[2])
    own_mix.start()
    for copy in mix_copies:
        copy.start()

    own_cot.wait()
    all_cot.wait()

    for k in (3, 2, 1, 0):
        for i in range(8):
            low, high = low_high(k, i)
            rows = pl.ds(i * CH, CH)
            gpv[rows, :D] = gs[low]
            gpv[rows, D:] = gs[high]
        mine = slice(k * ROWS, (k + 1) * ROWS)
        for j in range(FF // TILE):
            cols = slice(j * TILE, (j + 1) * TILE)
            d_hidden = dot_nn(gpv[...], wd[:, cols])
            rk[0, mine, cols] = (d_hidden * slope[k, :, cols]).astype(BF)
            if j < 3:
                part = slice(j * TILE, (j + 1) * TILE)
                lk[1, part, mine] = gpv[:, part].T

        @pl.when(c == 0)
        def _():
            send_left(k).start()

        @pl.when(c == 1)
        def _():
            send_right(k).start()

        if k > 0:
            for j in range(D2 // TILE):
                cols = slice(j * TILE, (j + 1) * TILE)
                acc[:, cols] = dot_nt(rk[0, k * ROWS : (k + 1) * ROWS], wu[cols])
            for i in range(8):
                low, high = low_high(k, i)
                rows = pl.ds(i * CH, CH)
                d_norm = acc[rows]
                normed = nf[k, rows]
                first = jnp.mean(d_norm, axis=-1, keepdims=True)
                second = jnp.mean(d_norm * normed, axis=-1, keepdims=True)
                d_pair = rs[k, rows] * (d_norm - first - normed * second)
                gs[low] = (gs[low].astype(F32) + d_pair[:, :D]).astype(BF)
                gs[high] = (gs[high].astype(F32) + d_pair[:, D:]).astype(BF)

    for k in range(4):
        send_left(k).wait()
        send_right(k).wait()

    count = [0]

    def link(src, dst, dev):
        n = count[0]
        count[0] += 1
        return remote(src, dst, red_s.at[n], red_r.at[n], dev)

    def mrow(group_y, half):
        return pl.ds(pl.multiple_of(group_y * 192 + half * 96, 48), 96)

    def hrow(group_y, part):
        return pl.ds(pl.multiple_of(group_y * 192 + part * 48, 48), 48)

    def span(first, size=48):
        return pl.ds(first * 48, size)

    a1 = [[link(sa1.at[i, d], ra1.at[i, d], ydev[d]) for d in range(2)] for i in range(4)]
    a2 = [
        [[link(sa2.at[i, d, span(h)], ra2.at[i, d, span(h)], ydev[d]) for h in range(2)] for d in range(2)]
        for i in range(4)
    ]
    x1 = [link(sx1.at[d], rx1.at[d], xdev[d]) for d in range(2)]
    x2 = [[link(sx2.at[d, span(h)], rx2.at[d, span(h)], xdev[d]) for h in range(2)] for d in range(2)]
    b1 = [[link(sb1.at[d, g], rb1.at[d, g], xdev[d]) for g in range(4)] for d in range(2)]
    b2 = [
        [[link(sb2.at[d, g, span(h)], rb2.at[d, g, span(h)], xdev[d]) for h in range(2)] for g in range(4)]
        for d in range(2)
    ]
    y1c = [link(sy1.at[d], ry1.at[d], ydev[d]) for d in range(2)]
    y2c = [[link(sy2.at[d, span(h)], ry2.at[d, span(h)], ydev[d]) for h in range(2)] for d in range(2)]
    near = (yp, ym)
    order = (y2, yp, ym, y)

    def unit_cols(i, first, size):
        xt = (x + (2, 1, 3, 0)[i]) % 4
        return pl.ds(pl.multiple_of(xt * 384 + first, 128), size)

    def wide(i):
        def body(t, carry):
            rows = pl.ds(pl.multiple_of(t * 256, 256), 256)
            m4[i, rows, :256] = dot_nn(lk[c, rows], rk[c, :, unit_cols(i, 0, 256)])
            return carry

        lax.fori_loop(0, 3, body, 0)

    def shared(i):
        def body(t, carry):
            rows = pl.ds(pl.multiple_of(t * 256, 256), 256)
            right = jnp.concatenate(
                [rk[c, :, unit_cols(i, 256, 128)], rk[c, :, unit_cols(i + 1, 256, 128)]], axis=1
            )
            out = dot_nn(lk[c, rows], right)
            m4[i, rows, 256:] = out[:, :128]
            m4[i + 1, rows, 256:] = out[:, 128:]
            return carry

        lax.fori_loop(0, 3, body, 0)

    def a_open(i):
        for d in range(2):
            sa1[i, d] = m4[i, hrow(y2, d)].astype(BF)
            a1[i][d].start()
        for d in range(2):
            sa2[i, d, (1 - d) * 48 : (2 - d) * 48] = m4[i, hrow(near[d], 1 - d)].astype(BF)
            a2[i][d][1 - d].start()

    def a_pass(i):
        for d in range(2):
            a1[i][d].wait()
            sa2[i, d, d * 48 : (d + 1) * 48] = (m4[i, hrow(near[d], d)] + ra1[i, d].astype(F32)).astype(BF)
            a2[i][d][d].start()

    def a_final(i):
        for d in range(2):
            a2[i][d][1 - d].wait()
            a2[i][d][d].wait()
        ay[i] = m4[i, mrow(y, 0)] + ra2[i, 0].astype(F32) + ra2[i, 1].astype(F32)

    def b_open():
        for g in range(4):
            for d in range(2):
                sb1[d, g] = m4[0, hrow(order[g], 2 + d)].astype(BF)
                b1[d][g].start()

    def b_free(d, g):
        free = slice((1 - d) * 48, (2 - d) * 48)
        sb2[d, g, free] = m4[1 + d, hrow(order[g], 3 - d)].astype(BF)
        b2[d][g][1 - d].start()

    def b_pass(d, g):
        held = slice(d * 48, (d + 1) * 48)
        b1[d][g].wait()
        sb2[d, g, held] = (m4[1 + d, hrow(order[g], 2 + d)] + rb1[d, g].astype(F32)).astype(BF)
        b2[d][g][d].start()

    def b_final(g):
        for d in range(2):
            b2[d][g][1 - d].wait()
            b2[d][g][d].wait()
        bx[g] = m4[3, mrow(order[g], 1)] + rb2[0, g].astype(F32) + rb2[1, g].astype(F32)

    def open_last(first, value, staged):
        for d in range(2):
            staged[d] = value[0, d * 48 : (d + 1) * 48].astype(BF)
            first[d].start()

    def pass_last(d, first, second, value, staged, got):
        free = slice((1 - d) * 48, (2 - d) * 48)
        held = slice(d * 48, (d + 1) * 48)
        staged[d, free] = value[1 + d, free].astype(BF)
        second[d][1 - d].start()
        first[d].wait()
        staged[d, held] = (value[1 + d, held] + got[d].astype(F32)).astype(BF)
        second[d][d].start()

    wide(0)
    shared(0)
    b_open()
    a_open(0)
    wide(1)
    b_free(0, 0)
    b_free(0, 1)
    a_open(1)
    wide(2)
    b_pass(0, 0)
    b_free(0, 2)
    b_pass(0, 1)
    b_free(0, 3)
    a_pass(0)
    shared(2)
    b_free(1, 0)
    b_pass(1, 0)
    b_free(1, 1)
    b_pass(1, 1)
    a_open(2)
    b_pass(0, 2)
    b_pass(0, 3)
    b_free(1, 2)
    b_pass(1, 2)
    b_free(1, 3)
    b_pass(1, 3)
    a_pass(1)
    wide(3)
    a_open(3)
    a_pass(2)
    a_final(0)
    open_last(x1, ay, sx1)
    b_final(0)
    open_last(y1c, bx, sy1)
    a_final(1)
    b_final(1)
    a_pass(3)
    pass_last(0, y1c, y2c, bx, sy2, ry1)
    pass_last(0, x1, x2, ay, sx2, rx1)
    a_final(2)
    pass_last(1, x1, x2, ay, sx2, rx1)
    b_final(2)
    pass_last(1, y1c, y2c, bx, sy2, ry1)
    b_final(3)
    a_final(3)

    z_copies = []
    for d in range(1, 8):
        zd = (z + d) % 8
        rows = pl.ds(pl.multiple_of((zd // 2) * 48, 48), 48)
        cols = pl.ds(pl.multiple_of((zd % 2) * 128, 128), 256)
        z_copies.append((zd, link(fz.at[rows, cols], zr.at[d - 1], zdev[d - 1])))

    def z_send(part):
        for zd, copy in z_copies:

            @pl.when(zd // 4 == part)
            def _():
                copy.start()

    for d in range(2):
        x2[d][1 - d].wait()
        x2[d][d].wait()
    ft[:96] = ay[3] + rx2[0].astype(F32) + rx2[1].astype(F32)
    fz[:96] = ft[:96].astype(BF)
    z_send(0)
    for d in range(2):
        y2c[d][1 - d].wait()
        y2c[d][d].wait()
    ft[96:] = bx[3] + ry2[0].astype(F32) + ry2[1].astype(F32)
    fz[96:] = ft[96:].astype(BF)
    z_send(1)
    rows = pl.ds(pl.multiple_of(zh * 48, 48), 48)
    cols = pl.ds(pl.multiple_of(zl * 128, 128), 256)
    total = ft[rows, cols]
    for d in range(7):
        z_copies[d][1].wait()
        total = total + zr[d].astype(F32)
    tt[...] = total
    last = link(tt, pt, other)
    last.start()
    gout[c] = total
    last.wait()
    gout[1 - c] = pt[...]

    own_mix.wait()
    all_mix.wait()


def finish(mixed, grads, mixed_out, up_out, down_out):
    gy = lax.axis_index("gy")
    start = (gy // 2) % 2 * 64 + gy % 2 * 96
    mixed_out[...] = mixed[...]
    for i, out in enumerate((up_out, down_out)):
        out[...] = pltpu.roll(grads[i], (256 - start) % 256, 1)[:, :96]


def local(signal, w_up, w_down, cotangent):
    vm = pltpu.VMEM
    dma = pltpu.SemaphoreType.DMA
    anyspec = pl.BlockSpec(memory_space=pl.ANY)
    mixed, grads = pl.pallas_call(
        kernel,
        out_shape=(
            jax.ShapeDtypeStruct((512, D), BF),
            jax.ShapeDtypeStruct((2, 48, 256), F32),
        ),
        in_specs=[anyspec] * 4,
        out_specs=(anyspec, pl.BlockSpec(memory_space=pltpu.VMEM)),
        scratch_shapes=[
            vm((16, CH, D), BF), vm((16, CH, D), BF), vm((ROWS, D2), BF), vm((ROWS, D2), BF),
            vm((4, ROWS, D2), F32), vm((4, ROWS, 1), F32), vm((4, ROWS, FF), F32), vm((ROWS, FF), F32),
            vm((D2, FF), BF), vm((D2, FF), BF), vm((ROWS, D2), F32),
            vm((2, D2, 8 * ROWS), BF), vm((2, 8 * ROWS, FF), BF),
            vm((4, D2, D), F32), vm((4, 96, D), F32), vm((4, 96, D), F32),
            vm((192, D), BF), vm((192, D), F32),
            vm((4, 2, 48, D), BF), vm((4, 2, 48, D), BF),
            vm((4, 2, 96, D), BF), vm((4, 2, 96, D), BF),
            vm((2, 48, D), BF), vm((2, 48, D), BF), vm((2, 96, D), BF), vm((2, 96, D), BF),
            vm((2, 4, 48, D), BF), vm((2, 4, 48, D), BF),
            vm((2, 4, 96, D), BF), vm((2, 4, 96, D), BF),
            vm((2, 48, D), BF), vm((2, 48, D), BF), vm((2, 96, D), BF), vm((2, 96, D), BF),
            vm((7, 48, 256), BF), vm((48, 256), F32), vm((48, 256), F32),
            dma((1,)), dma((1,)), dma((1,)), dma((1,)), dma((1,)), dma((1,)),
            dma((4,)), dma((4,)), dma((4,)), dma((4,)), dma((4,)),
            dma((68,)), dma((68,)),
        ],
        compiler_params=pltpu.CompilerParams(
            collective_id=0, has_side_effects=True, vmem_limit_bytes=62 << 20
        ),
    )(signal, cotangent, w_up, w_down)
    return pl.pallas_call(
        finish,
        out_shape=(
            jax.ShapeDtypeStruct((512, D), BF),
            jax.ShapeDtypeStruct((48, 96), F32),
            jax.ShapeDtypeStruct((48, 96), F32),
        ),
        in_specs=[pl.BlockSpec(memory_space=pltpu.VMEM)] * 2,
        out_specs=(pl.BlockSpec(memory_space=pltpu.VMEM),) * 3,
    )(mixed, grads)


def solution(mesh):
    return jax.shard_map(
        local,
        mesh=mesh,
        in_specs=(P(("gx", "gy"), None), P(), P(), P(("gx", "gy"), None)),
        out_specs=(P(("gx", "gy"), None), P("gx", "gy"), P("gx", "gy")),
        check_vma=False,
    )
```

```python
import math

import jax
import jax.numpy as jnp
from jax import lax
from jax.experimental import pallas as pl
from jax.experimental.pallas import tpu as pltpu
from jax.sharding import PartitionSpec as P

MESH = pl.DeviceIdType.MESH
BF = jnp.bfloat16
F32 = jnp.float32
D = 384
D2 = 768
FF = 1536
CH = 32
ROWS = 256
TILE = 256


def dot_nn(left, right):
    return lax.dot_general(left, right, (((1,), (0,)), ((), ())), preferred_element_type=F32)


def dot_nt(left, right):
    return lax.dot_general(left, right, (((1,), (1,)), ((), ())), preferred_element_type=F32)


def kernel(
    sig, cot, wu_hbm, wd_hbm, mixed, gout,
    xs, gs, nbv, gpv, nf, rs, slope, prev, wu, wd, acc, lk, rk, m4, ay, bx, fz, ft,
    sa1, ra1, sa2, ra2, sx1, rx1, sx2, rx2, sb1, rb1, sb2, rb2, sy1, ry1, sy2, ry2, zr, pt, tt,
    sig_s, sig_r, cot_s, cot_r, mix_s, mix_r, loc, lk_s, lk_r, rk_s, rk_r, red_s, red_r,
):
    gx = lax.axis_index("gx")
    gy = lax.axis_index("gy")
    y, zh = gx // 4, gx % 4
    x, zl, c = gy // 4, (gy // 2) % 2, gy % 2
    z = zh * 2 + zl
    ba, bb, bc = y // 2, zh % 2, x // 2
    me = ba * 8 + bb * 4 + bc * 2 + c

    def at(xx, yy, zz, cc):
        return {"gx": yy * 4 + zz // 2, "gy": xx * 4 + (zz % 2) * 2 + cc}

    yp, ym, y2 = (y + 1) % 4, (y + 3) % 4, (y + 2) % 4
    xp, xm = (x + 1) % 4, (x + 3) % 4
    ydev = (at(x, yp, z, c), at(x, ym, z, c))
    xdev = (at(xp, y, z, c), at(xm, y, z, c))
    zdev = [at(x, y, (z + d) % 8, c) for d in range(1, 8)]
    other = at(x, y, z, 1 - c)
    group = []
    for r in range(1, 16):
        ra, rb, rc, rd = r // 8, (r // 4) % 2, (r // 2) % 2, r % 2
        yy = y + ra * (2 - 4 * ba)
        zz = z + rb * (2 - 4 * bb)
        xx = x + rc * (2 - 4 * bc)
        cc = c + rd * (1 - 2 * c)
        target = (yy // 2) * 8 + ((zz // 2) % 2) * 4 + (xx // 2) * 2 + cc
        group.append((r, at(xx, yy, zz, cc), target))

    load_wu = pltpu.make_async_copy(wu_hbm, wu, loc.at[0])
    load_wd = pltpu.make_async_copy(wd_hbm, wd, loc.at[1])
    load_wu.start()
    load_wd.start()
    own_rows = pl.ds(pl.multiple_of(me * CH, CH), CH)
    own_sig = pltpu.make_async_copy(sig.at[own_rows], xs.at[me], loc.at[2])
    own_cot = pltpu.make_async_copy(cot.at[own_rows], gs.at[me], loc.at[3])
    own_sig.start()
    own_cot.start()

    barrier = pltpu.get_barrier_semaphore()
    peers = [dev for _, dev, _ in group] + zdev + list(ydev) + list(xdev)
    for dev in peers:
        pl.semaphore_signal(barrier, inc=1, device_id=dev, device_id_type=MESH)
    pl.semaphore_wait(barrier, len(peers))

    def remote(src, dst, send, recv, dev):
        return pltpu.make_async_remote_copy(
            src_ref=src, dst_ref=dst, send_sem=send, recv_sem=recv, device_id=dev, device_id_type=MESH
        )

    sig_copies, cot_copies = [], []
    for r, dev, target in reversed(group):
        rows = pl.ds(pl.multiple_of(target * CH, CH), CH)
        sig_copies.append(remote(sig.at[rows], xs.at[me], sig_s.at[0], sig_r.at[0], dev))
        cot_copies.append(remote(cot.at[rows], gs.at[me], cot_s.at[0], cot_r.at[0], dev))
    for copy in sig_copies:
        copy.start()
    load_wu.wait()
    load_wd.wait()
    own_sig.wait()
    most = pl.ds(0, 15)
    wide_rows = pl.ds(0, 15 * CH)
    all_sig = remote(sig.at[wide_rows], xs.at[most], sig_s.at[0], sig_r.at[0], other)
    all_cot = remote(cot.at[wide_rows], gs.at[most], cot_s.at[0], cot_r.at[0], other)
    all_mix = remote(xs.at[most], mixed.at[wide_rows], mix_s.at[0], mix_r.at[0], other)
    all_sig.wait()
    for copy in cot_copies:
        copy.start()

    def low_high(k, i):
        stride = 8 >> k
        low = (i // stride) * 2 * stride + i % stride
        return low, low + stride

    def store_turned(which, t, mine, source):
        turned = source[:, t * TILE : (t + 1) * TILE].T
        for b in range(TILE // 16):
            block = t * (TILE // 16) + b
            group_y, inner = block // 12, block % 12
            zz, third = inner // 3, inner % 3
            odd = zz % 2
            spot = (3 * (zz // 2) + (2 * odd, 1 + 6 * odd, 6 + 2 * odd)[third]) * 16 + group_y * 192
            lk[which, spot : spot + 16, mine] = turned[b * 16 : (b + 1) * 16]

    def send_left(k):
        cols = pl.ds(k * ROWS, ROWS)
        into = pl.ds(4 * ROWS + k * ROWS, ROWS)
        return remote(lk.at[1 - c, :, cols], lk.at[1 - c, :, into], lk_s.at[k], lk_r.at[k], other)

    def send_right(k):
        cols = pl.ds(k * ROWS, ROWS)
        into = pl.ds(4 * ROWS + k * ROWS, ROWS)
        return remote(rk.at[1 - c, cols], rk.at[1 - c, into], rk_s.at[k], rk_r.at[k], other)

    for k in range(4):
        for i in range(8):
            low, high = low_high(k, i)
            rows = pl.ds(i * CH, CH)
            pair = jnp.concatenate([xs[low], xs[high]], axis=1).astype(F32)
            centre = jnp.mean(pair, axis=-1, keepdims=True)
            shifted = pair - centre
            spread = jnp.mean(shifted * shifted, axis=-1, keepdims=True)
            factor = lax.rsqrt(spread + 1e-05)
            normed = shifted * factor
            nf[k, rows] = normed
            rs[k, rows] = factor
            nbv[rows] = normed.astype(BF)
        mine = slice(k * ROWS, (k + 1) * ROWS)
        for j in range(FF // TILE):
            cols = slice(j * TILE, (j + 1) * TILE)
            pre = dot_nn(nbv[...], wu[:, cols])
            half = 0.5 + 0.5 * lax.erf(pre * (1.0 / math.sqrt(2.0)))
            rk[1, mine, cols] = (pre * half).astype(BF)
            prev[:, cols] = pre
            slope[k, :, cols] = half
            if j % 2 == 1:
                store_turned(0, j // 2, mine, nbv)

        @pl.when(c == 0)
        def _():
            send_right(k).start()

        for j in range(D2 // TILE):
            cols = slice(j * TILE, (j + 1) * TILE)
            out = dot_nt(rk[1, mine], wd[cols])
            for i in range(8):
                low, high = low_high(k, i)
                for at_pos, first in ((low, 0), (high, D)):
                    lo, hi = max(first, j * TILE), min(first + D, (j + 1) * TILE)
                    if lo < hi:
                        here = slice(lo - first, hi - first)
                        value = out[i * CH : (i + 1) * CH, lo - j * TILE : hi - j * TILE]
                        xs[at_pos, :, here] = (xs[at_pos, :, here].astype(F32) + value).astype(BF)
            for t in (2 * j, 2 * j + 1):
                cols = slice(t * TILE, (t + 1) * TILE)
                pre = prev[:, cols]
                bell = jnp.exp2(pre * pre * (-0.5 * math.log2(math.e)))
                slope[k, :, cols] = slope[k, :, cols] + pre * (1.0 / math.sqrt(2.0 * math.pi)) * bell

        @pl.when(c == 1)
        def _():
            send_left(k).start()

    mix_copies = []
    for r, dev, target in group:
        mix_copies.append(remote(xs.at[target], mixed.at[own_rows], mix_s.at[0], mix_r.at[0], dev))
    own_mix = pltpu.make_async_copy(xs.at[me], mixed.at[own_rows], loc.at[2])
    own_mix.start()
    for copy in mix_copies:
        copy.start()

    own_cot.wait()
    all_cot.wait()

    for k in (3, 2, 1, 0):
        for i in range(8):
            low, high = low_high(k, i)
            rows = pl.ds(i * CH, CH)
            gpv[rows, :D] = gs[low]
            gpv[rows, D:] = gs[high]
        mine = slice(k * ROWS, (k + 1) * ROWS)
        for j in range(FF // TILE):
            cols = slice(j * TILE, (j + 1) * TILE)
            d_hidden = dot_nn(gpv[...], wd[:, cols])
            rk[0, mine, cols] = (d_hidden * slope[k, :, cols]).astype(BF)
            if j < 3:
                store_turned(1, j, mine, gpv)

        @pl.when(c == 0)
        def _():
            send_left(k).start()

        @pl.when(c == 1)
        def _():
            send_right(k).start()

        if k > 0:
            for j in range(D2 // TILE):
                cols = slice(j * TILE, (j + 1) * TILE)
                acc[:, cols] = dot_nt(rk[0, k * ROWS : (k + 1) * ROWS], wu[cols])
            for i in range(8):
                low, high = low_high(k, i)
                rows = pl.ds(i * CH, CH)
                d_norm = acc[rows]
                normed = nf[k, rows]
                first = jnp.mean(d_norm, axis=-1, keepdims=True)
                second = jnp.mean(d_norm * normed, axis=-1, keepdims=True)
                d_pair = rs[k, rows] * (d_norm - first - normed * second)
                gs[low] = (gs[low].astype(F32) + d_pair[:, :D]).astype(BF)
                gs[high] = (gs[high].astype(F32) + d_pair[:, D:]).astype(BF)

    for k in range(4):
        send_left(k).wait()
        send_right(k).wait()

    count = [0]

    def fresh():
        count[0] += 1
        return count[0] - 1

    def link(src, dst, dev, n=None):
        n = fresh() if n is None else n
        return remote(src, dst, red_s.at[n], red_r.at[n], dev)

    def mrow(group_y, half):
        return pl.ds(pl.multiple_of(group_y * 192 + half * 96, 48), 96)

    def hrow(group_y, part):
        return pl.ds(pl.multiple_of(group_y * 192 + part * 48, 48), 48)

    def span(first, size=48):
        return pl.ds(first * 48, size)

    a1 = [[link(sa1.at[i, d], ra1.at[i, d], ydev[d]) for d in range(2)] for i in range(4)]
    a2n = [fresh() for i in range(4)]
    a2 = [
        [[link(sa2.at[i, d, span(h)], ra2.at[i, d, span(h)], ydev[d], a2n[i]) for h in range(2)] for d in range(2)]
        for i in range(4)
    ]
    a2_all = [link(sa2.at[i], ra2.at[i], ydev[0], a2n[i]) for i in range(4)]
    x1 = [link(sx1.at[d], rx1.at[d], xdev[d]) for d in range(2)]
    x2n, y2n, zn = fresh(), fresh(), fresh()
    x2 = [[link(sx2.at[d, span(h)], rx2.at[d, span(h)], xdev[d], x2n) for h in range(2)] for d in range(2)]
    x2_all = link(sx2, rx2, xdev[0], x2n)
    b1 = [[link(sb1.at[d, g], rb1.at[d, g], xdev[d]) for g in range(4)] for d in range(2)]
    b2n = [fresh() for g in range(4)]
    b2 = [
        [[link(sb2.at[d, g, span(h)], rb2.at[d, g, span(h)], xdev[d], b2n[g]) for h in range(2)] for g in range(4)]
        for d in range(2)
    ]
    b2_all = [link(sb2.at[:, g], rb2.at[:, g], xdev[0], b2n[g]) for g in range(4)]
    y1c = [link(sy1.at[d], ry1.at[d], ydev[d]) for d in range(2)]
    y2c = [[link(sy2.at[d, span(h)], ry2.at[d, span(h)], ydev[d], y2n) for h in range(2)] for d in range(2)]
    y2_all = link(sy2, ry2, ydev[0], y2n)
    near = (yp, ym)
    order = (y2, yp, ym, y)

    def unit_cols(i, first, size):
        xt = (x + (2, 1, 3, 0)[i]) % 4
        return pl.ds(pl.multiple_of(xt * 384 + first, 128), size)

    def wide(i):
        m4[i, :, :256] = dot_nn(lk[c], rk[c, :, unit_cols(i, 0, 256)])

    def shared(i):
        right = jnp.concatenate(
            [rk[c, :, unit_cols(i, 256, 128)], rk[c, :, unit_cols(i + 1, 256, 128)]], axis=1
        )
        out = dot_nn(lk[c], right)
        m4[i, :, 256:] = out[:, :128]
        m4[i + 1, :, 256:] = out[:, 128:]

    def a_open(i):
        for d in range(2):
            sa1[i, d] = m4[i, hrow(y2, d)].astype(BF)
            a1[i][d].start()
        for d in range(2):
            sa2[i, d, (1 - d) * 48 : (2 - d) * 48] = m4[i, hrow(near[d], 1 - d)].astype(BF)
            a2[i][d][1 - d].start()

    def a_pass(i):
        for d in range(2):
            a1[i][d].wait()
            sa2[i, d, d * 48 : (d + 1) * 48] = (m4[i, hrow(near[d], d)] + ra1[i, d].astype(F32)).astype(BF)
            a2[i][d][d].start()

    def a_final(i):
        a2_all[i].wait()
        ay[i] = m4[i, mrow(y, 0)] + ra2[i, 0].astype(F32) + ra2[i, 1].astype(F32)

    def b_open():
        for g in range(4):
            for d in range(2):
                sb1[d, g] = m4[0, hrow(order[g], 2 + d)].astype(BF)
                b1[d][g].start()

    def b_free(d, g):
        free = slice((1 - d) * 48, (2 - d) * 48)
        sb2[d, g, free] = m4[1 + d, hrow(order[g], 3 - d)].astype(BF)
        b2[d][g][1 - d].start()

    def b_pass(d, g):
        held = slice(d * 48, (d + 1) * 48)
        b1[d][g].wait()
        sb2[d, g, held] = (m4[1 + d, hrow(order[g], 2 + d)] + rb1[d, g].astype(F32)).astype(BF)
        b2[d][g][d].start()

    def b_final(g):
        b2_all[g].wait()
        bx[g] = m4[3, mrow(order[g], 1)] + rb2[0, g].astype(F32) + rb2[1, g].astype(F32)

    def open_last(first, value, staged):
        for d in range(2):
            staged[d] = value[0, d * 48 : (d + 1) * 48].astype(BF)
            first[d].start()

    def pass_last(d, first, second, value, staged, got):
        free = slice((1 - d) * 48, (2 - d) * 48)
        held = slice(d * 48, (d + 1) * 48)
        staged[d, free] = value[1 + d, free].astype(BF)
        second[d][1 - d].start()
        first[d].wait()
        staged[d, held] = (value[1 + d, held] + got[d].astype(F32)).astype(BF)
        second[d][d].start()

    wide(0)
    shared(0)
    b_open()
    a_open(0)
    wide(1)
    b_free(0, 0)
    b_free(0, 1)
    a_open(1)
    wide(2)
    b_pass(0, 0)
    b_free(0, 2)
    b_pass(0, 1)
    a_pass(0)
    shared(2)
    b_free(1, 0)
    b_pass(1, 0)
    b_free(1, 1)
    b_pass(1, 1)
    a_open(2)
    b_pass(0, 2)
    b_free(1, 2)
    b_pass(1, 2)
    a_pass(1)
    wide(3)
    a_open(3)
    a_pass(2)
    a_final(0)
    open_last(x1, ay, sx1)
    b_final(0)
    open_last(y1c, bx, sy1)
    a_final(1)
    pass_last(0, x1, x2, ay, sx2, rx1)
    b_free(0, 3)
    b_pass(0, 3)
    a_pass(3)
    b_final(1)
    pass_last(0, y1c, y2c, bx, sy2, ry1)
    a_final(2)
    pass_last(1, x1, x2, ay, sx2, rx1)
    b_free(1, 3)
    b_pass(1, 3)
    b_final(2)
    pass_last(1, y1c, y2c, bx, sy2, ry1)
    a_final(3)

    def third_rows(zz, third):
        base, odd = (zz // 2) * 48, zz % 2
        first = (base + odd * 32, base + 16 + odd * 96, base + 96 + odd * 32)[third]
        return pl.ds(pl.multiple_of(first, 16), 16)

    z_copies = []
    for d in (4, 3, 5, 2, 6, 1, 7):
        zd = (z + d) % 8
        cols = pl.ds(pl.multiple_of((zd % 2) * 128, 128), 256)
        pieces = [
            link(fz.at[third_rows(zd // 2, t), cols], zr.at[d - 1, pl.ds(t * 16, 16)], zdev[d - 1], zn)
            for t in range(3)
        ]
        z_copies.append((zd, pieces))

    def z_send(part):
        for zd, pieces in z_copies:
            pieces[2 * part].start()

            @pl.when((zd // 2) % 2 == part)
            def _():
                pieces[1].start()

    x2_all.wait()
    ft[:96] = ay[3] + rx2[0].astype(F32) + rx2[1].astype(F32)
    fz[:96] = ft[:96].astype(BF)
    z_send(0)
    b_final(3)
    y2_all.wait()
    ft[96:] = bx[3] + ry2[0].astype(F32) + ry2[1].astype(F32)
    fz[96:] = ft[96:].astype(BF)
    z_send(1)
    cols = pl.ds(pl.multiple_of(zl * 128, 128), 256)
    total = jnp.concatenate([ft[third_rows(zh, t), cols] for t in range(3)], axis=0)
    link(zr, zr, zdev[0], zn).wait()
    for d in range(7):
        total = total + zr[d].astype(F32)
    tt[...] = total
    last = link(tt, pt, other)
    last.start()
    gout[c] = total
    last.wait()
    gout[1 - c] = pt[...]

    own_mix.wait()
    all_mix.wait()


def finish(mixed, grads, mixed_out, up_out, down_out):
    gy = lax.axis_index("gy")
    start = (gy // 2) % 2 * 64 + gy % 2 * 96
    mixed_out[...] = mixed[...]
    for i, out in enumerate((up_out, down_out)):
        out[...] = pltpu.roll(grads[i], (256 - start) % 256, 1)[:, :96]


def local(signal, w_up, w_down, cotangent):
    vm = pltpu.VMEM
    dma = pltpu.SemaphoreType.DMA
    anyspec = pl.BlockSpec(memory_space=pl.ANY)
    mixed, grads = pl.pallas_call(
        kernel,
        out_shape=(
            jax.ShapeDtypeStruct((512, D), BF),
            jax.ShapeDtypeStruct((2, 48, 256), F32),
        ),
        in_specs=[anyspec] * 4,
        out_specs=(anyspec, pl.BlockSpec(memory_space=pltpu.VMEM)),
        scratch_shapes=[
            vm((16, CH, D), BF), vm((16, CH, D), BF), vm((ROWS, D2), BF), vm((ROWS, D2), BF),
            vm((4, ROWS, D2), F32), vm((4, ROWS, 1), F32), vm((4, ROWS, FF), F32), vm((ROWS, FF), F32),
            vm((D2, FF), BF), vm((D2, FF), BF), vm((ROWS, D2), F32),
            vm((2, D2, 8 * ROWS), BF), vm((2, 8 * ROWS, FF), BF),
            vm((4, D2, D), F32), vm((4, 96, D), F32), vm((4, 96, D), F32),
            vm((192, D), BF), vm((192, D), F32),
            vm((4, 2, 48, D), BF), vm((4, 2, 48, D), BF),
            vm((4, 2, 96, D), BF), vm((4, 2, 96, D), BF),
            vm((2, 48, D), BF), vm((2, 48, D), BF), vm((2, 96, D), BF), vm((2, 96, D), BF),
            vm((2, 4, 48, D), BF), vm((2, 4, 48, D), BF),
            vm((2, 4, 96, D), BF), vm((2, 4, 96, D), BF),
            vm((2, 48, D), BF), vm((2, 48, D), BF), vm((2, 96, D), BF), vm((2, 96, D), BF),
            vm((7, 48, 256), BF), vm((48, 256), F32), vm((48, 256), F32),
            dma((1,)), dma((1,)), dma((1,)), dma((1,)), dma((1,)), dma((1,)),
            dma((4,)), dma((4,)), dma((4,)), dma((4,)), dma((4,)),
            dma((32,)), dma((32,)),
        ],
        compiler_params=pltpu.CompilerParams(
            collective_id=0, has_side_effects=True, vmem_limit_bytes=62 << 20
        ),
    )(signal, cotangent, w_up, w_down)
    return pl.pallas_call(
        finish,
        out_shape=(
            jax.ShapeDtypeStruct((512, D), BF),
            jax.ShapeDtypeStruct((48, 96), F32),
            jax.ShapeDtypeStruct((48, 96), F32),
        ),
        in_specs=[pl.BlockSpec(memory_space=pltpu.VMEM)] * 2,
        out_specs=(pl.BlockSpec(memory_space=pltpu.VMEM),) * 3,
    )(mixed, grads)


def solution(mesh):
    return jax.shard_map(
        local,
        mesh=mesh,
        in_specs=(P(("gx", "gy"), None), P(), P(), P(("gx", "gy"), None)),
        out_specs=(P(("gx", "gy"), None), P("gx", "gy"), P("gx", "gy")),
        check_vma=False,
    )
```

```python
import math

import jax
import jax.numpy as jnp
from jax import lax
from jax.experimental import pallas as pl
from jax.experimental.pallas import tpu as pltpu
from jax.sharding import PartitionSpec as P

MESH = pl.DeviceIdType.MESH
BF = jnp.bfloat16
F32 = jnp.float32
D = 384
D2 = 768
FF = 1536
CH = 32
ROWS = 256
TILE = 256


def dot_nn(left, right):
    return lax.dot_general(left, right, (((1,), (0,)), ((), ())), preferred_element_type=F32)


def dot_nt(left, right):
    return lax.dot_general(left, right, (((1,), (1,)), ((), ())), preferred_element_type=F32)


def kernel(
    sig, cot, wu_hbm, wd_hbm, mixed, gout,
    xs, gs, nbv, gpv, nf, rs, slope, prev, wu, wd, acc, lk, rk, m4, ay, bx, fz, ft,
    sa1, ra1, sa2, ra2, sx1, rx1, sx2, rx2, sb1, rb1, sb2, rb2, sy1, ry1, sy2, ry2, zr, pt, tt,
    sig_s, sig_r, cot_s, cot_r, mix_s, mix_r, loc, lk_s, lk_r, rk_s, rk_r, red_s, red_r,
):
    gx = lax.axis_index("gx")
    gy = lax.axis_index("gy")
    y, zh = gx // 4, gx % 4
    x, zl, c = gy // 4, (gy // 2) % 2, gy % 2
    z = zh * 2 + zl
    ba, bb, bc = y // 2, zh % 2, x // 2
    me = ba * 8 + bb * 4 + bc * 2 + c

    def at(xx, yy, zz, cc):
        return {"gx": yy * 4 + zz // 2, "gy": xx * 4 + (zz % 2) * 2 + cc}

    yp, ym, y2 = (y + 1) % 4, (y + 3) % 4, (y + 2) % 4
    xp, xm = (x + 1) % 4, (x + 3) % 4
    ydev = (at(x, yp, z, c), at(x, ym, z, c))
    xdev = (at(xp, y, z, c), at(xm, y, z, c))
    zdev = [at(x, y, (z + d) % 8, c) for d in range(1, 8)]
    other = at(x, y, z, 1 - c)
    group = []
    for r in range(1, 16):
        ra, rb, rc, rd = r // 8, (r // 4) % 2, (r // 2) % 2, r % 2
        yy = y + ra * (2 - 4 * ba)
        zz = z + rb * (2 - 4 * bb)
        xx = x + rc * (2 - 4 * bc)
        cc = c + rd * (1 - 2 * c)
        target = (yy // 2) * 8 + ((zz // 2) % 2) * 4 + (xx // 2) * 2 + cc
        group.append((r, at(xx, yy, zz, cc), target))

    load_wu = pltpu.make_async_copy(wu_hbm, wu, loc.at[0])
    load_wd = pltpu.make_async_copy(wd_hbm, wd, loc.at[1])
    load_wu.start()
    load_wd.start()
    own_rows = pl.ds(pl.multiple_of(me * CH, CH), CH)
    own_sig = pltpu.make_async_copy(sig.at[own_rows], xs.at[me], loc.at[2])
    own_cot = pltpu.make_async_copy(cot.at[own_rows], gs.at[me], loc.at[3])
    own_sig.start()
    own_cot.start()

    barrier = pltpu.get_barrier_semaphore()
    peers = [dev for _, dev, _ in group] + zdev + list(ydev) + list(xdev)
    for dev in peers:
        pl.semaphore_signal(barrier, inc=1, device_id=dev, device_id_type=MESH)
    pl.semaphore_wait(barrier, len(peers))

    def remote(src, dst, send, recv, dev):
        return pltpu.make_async_remote_copy(
            src_ref=src, dst_ref=dst, send_sem=send, recv_sem=recv, device_id=dev, device_id_type=MESH
        )

    sig_copies, cot_copies = [], []
    for r, dev, target in reversed(group):
        rows = pl.ds(pl.multiple_of(target * CH, CH), CH)
        sig_copies.append(remote(sig.at[rows], xs.at[me], sig_s.at[0], sig_r.at[0], dev))
        cot_copies.append(remote(cot.at[rows], gs.at[me], cot_s.at[0], cot_r.at[0], dev))
    for copy in sig_copies:
        copy.start()
    load_wu.wait()
    load_wd.wait()
    own_sig.wait()
    most = pl.ds(0, 15)
    wide_rows = pl.ds(0, 15 * CH)
    all_sig = remote(sig.at[wide_rows], xs.at[most], sig_s.at[0], sig_r.at[0], other)
    all_cot = remote(cot.at[wide_rows], gs.at[most], cot_s.at[0], cot_r.at[0], other)
    all_mix = remote(xs.at[most], mixed.at[wide_rows], mix_s.at[0], mix_r.at[0], other)
    all_sig.wait()
    for copy in cot_copies:
        copy.start()

    def low_high(k, i):
        stride = 8 >> k
        low = (i // stride) * 2 * stride + i % stride
        return low, low + stride

    def store_turned(which, t, mine, source):
        turned = source[:, t * TILE : (t + 1) * TILE].T
        for b in range(TILE // 16):
            block = t * (TILE // 16) + b
            group_y, inner = block // 12, block % 12
            zz, third = inner // 3, inner % 3
            odd = zz % 2
            spot = (3 * (zz // 2) + (2 * odd, 1 + 6 * odd, 6 + 2 * odd)[third]) * 16 + group_y * 192
            lk[which, spot : spot + 16, mine] = turned[b * 16 : (b + 1) * 16]

    def send_left(k):
        cols = pl.ds(k * ROWS, ROWS)
        into = pl.ds(4 * ROWS + k * ROWS, ROWS)
        return remote(lk.at[1 - c, :, cols], lk.at[1 - c, :, into], lk_s.at[k], lk_r.at[k], other)

    def send_right(k):
        cols = pl.ds(k * ROWS, ROWS)
        into = pl.ds(4 * ROWS + k * ROWS, ROWS)
        return remote(rk.at[1 - c, cols], rk.at[1 - c, into], rk_s.at[k], rk_r.at[k], other)

    def send_right_part(p):
        cols = pl.ds(p * 512, 512)
        source = rk.at[1 - c, pl.ds(0, ROWS), cols]
        return remote(source, rk.at[1 - c, pl.ds(4 * ROWS, ROWS), cols], rk_s.at[0], rk_r.at[0], other)

    for k in range(4):
        for i in range(8):
            low, high = low_high(k, i)
            rows = pl.ds(i * CH, CH)
            pair = jnp.concatenate([xs[low], xs[high]], axis=1).astype(F32)
            centre = jnp.mean(pair, axis=-1, keepdims=True)
            shifted = pair - centre
            spread = jnp.mean(shifted * shifted, axis=-1, keepdims=True)
            factor = lax.rsqrt(spread + 1e-05)
            normed = shifted * factor
            nf[k, rows] = normed
            rs[k, rows] = factor
            nbv[rows] = normed.astype(BF)
        mine = slice(k * ROWS, (k + 1) * ROWS)
        for j in range(FF // TILE):
            cols = slice(j * TILE, (j + 1) * TILE)
            pre = dot_nn(nbv[...], wu[:, cols])
            half = 0.5 + 0.5 * lax.erf(pre * (1.0 / math.sqrt(2.0)))
            rk[1, mine, cols] = (pre * half).astype(BF)
            prev[:, cols] = pre
            slope[k, :, cols] = half
            if j % 2 == 1:
                store_turned(0, j // 2, mine, nbv)

        @pl.when(c == 0)
        def _():
            send_right(k).start()

        for j in range(D2 // TILE):
            cols = slice(j * TILE, (j + 1) * TILE)
            out = dot_nt(rk[1, mine], wd[cols])
            for i in range(8):
                low, high = low_high(k, i)
                for at_pos, first in ((low, 0), (high, D)):
                    lo, hi = max(first, j * TILE), min(first + D, (j + 1) * TILE)
                    if lo < hi:
                        here = slice(lo - first, hi - first)
                        value = out[i * CH : (i + 1) * CH, lo - j * TILE : hi - j * TILE]
                        xs[at_pos, :, here] = (xs[at_pos, :, here].astype(F32) + value).astype(BF)
            for t in (2 * j, 2 * j + 1):
                cols = slice(t * TILE, (t + 1) * TILE)
                pre = prev[:, cols]
                bell = jnp.exp2(pre * pre * (-0.5 * math.log2(math.e)))
                slope[k, :, cols] = slope[k, :, cols] + pre * (1.0 / math.sqrt(2.0 * math.pi)) * bell

        @pl.when(c == 1)
        def _():
            send_left(k).start()

    mix_copies = []
    for r, dev, target in group:
        mix_copies.append(remote(xs.at[target], mixed.at[own_rows], mix_s.at[0], mix_r.at[0], dev))
    own_mix = pltpu.make_async_copy(xs.at[me], mixed.at[own_rows], loc.at[2])
    own_mix.start()
    for copy in mix_copies:
        copy.start()

    own_cot.wait()
    all_cot.wait()

    for k in (3, 2, 1, 0):
        for i in range(8):
            low, high = low_high(k, i)
            rows = pl.ds(i * CH, CH)
            gpv[rows, :D] = gs[low]
            gpv[rows, D:] = gs[high]
        mine = slice(k * ROWS, (k + 1) * ROWS)
        if k == 0:
            for j in range(3):
                store_turned(1, j, mine, gpv)

            @pl.when(c == 0)
            def _():
                send_left(k).start()

        for j in range(FF // TILE):
            cols = slice(j * TILE, (j + 1) * TILE)
            d_hidden = dot_nn(gpv[...], wd[:, cols])
            rk[0, mine, cols] = (d_hidden * slope[k, :, cols]).astype(BF)
            if k > 0 and j < 3:
                store_turned(1, j, mine, gpv)
            if k == 0 and j % 2 == 1:

                @pl.when(c == 1)
                def _():
                    send_right_part(j // 2).start()

        if k > 0:

            @pl.when(c == 0)
            def _():
                send_left(k).start()

            @pl.when(c == 1)
            def _():
                send_right(k).start()

        if k > 0:
            for j in range(D2 // TILE):
                cols = slice(j * TILE, (j + 1) * TILE)
                acc[:, cols] = dot_nt(rk[0, k * ROWS : (k + 1) * ROWS], wu[cols])
            for i in range(8):
                low, high = low_high(k, i)
                rows = pl.ds(i * CH, CH)
                d_norm = acc[rows]
                normed = nf[k, rows]
                first = jnp.mean(d_norm, axis=-1, keepdims=True)
                second = jnp.mean(d_norm * normed, axis=-1, keepdims=True)
                d_pair = rs[k, rows] * (d_norm - first - normed * second)
                gs[low] = (gs[low].astype(F32) + d_pair[:, :D]).astype(BF)
                gs[high] = (gs[high].astype(F32) + d_pair[:, D:]).astype(BF)

    for k in range(4):
        send_left(k).wait()
        send_right(k).wait()

    count = [0]

    def fresh():
        count[0] += 1
        return count[0] - 1

    def link(src, dst, dev, n=None):
        n = fresh() if n is None else n
        return remote(src, dst, red_s.at[n], red_r.at[n], dev)

    def mrow(group_y, half):
        return pl.ds(pl.multiple_of(group_y * 192 + half * 96, 48), 96)

    def hrow(group_y, part):
        return pl.ds(pl.multiple_of(group_y * 192 + part * 48, 48), 48)

    def span(first, size=48):
        return pl.ds(first * 48, size)

    a1 = [None] + [[link(sa1.at[i, d], ra1.at[i, d], ydev[d]) for d in range(2)] for i in range(1, 4)]
    a2n = [fresh() for i in range(4)]
    a2 = [
        [[link(sa2.at[i, d, span(h)], ra2.at[i, d, span(h)], ydev[d], a2n[i]) for h in range(2)] for d in range(2)]
        for i in range(4)
    ]
    a2_all = [link(sa2.at[i], ra2.at[i], ydev[0], a2n[i]) for i in range(4)]
    x1 = [link(sx1.at[d], rx1.at[d], xdev[d]) for d in range(2)]
    x2n, y2n, zn = fresh(), fresh(), fresh()
    x2 = [[link(sx2.at[d, span(h)], rx2.at[d, span(h)], xdev[d], x2n) for h in range(2)] for d in range(2)]
    x2_all = link(sx2, rx2, xdev[0], x2n)
    parts = ((0, 256), (256, 128))

    def pieces_of(whole, src, dst, dev):
        n = fresh()
        whole.append(link(src, dst, dev, n))
        return [link(src.at[:, pl.ds(*p)], dst.at[:, pl.ds(*p)], dev, n) for p in parts]

    a1_first, b1, b1_parts = [], [[], []], []
    a1_parts = [pieces_of(a1_first, sa1.at[0, d], ra1.at[0, d], ydev[d]) for d in range(2)]
    a1[0] = a1_first
    for d in range(2):
        b1_parts.append([pieces_of(b1[d], sb1.at[d, g], rb1.at[d, g], xdev[d]) for g in range(4)])
    b2n = [fresh() for g in range(4)]
    b2 = [
        [[link(sb2.at[d, g, span(h)], rb2.at[d, g, span(h)], xdev[d], b2n[g]) for h in range(2)] for g in range(4)]
        for d in range(2)
    ]
    b2_all = [link(sb2.at[:, g], rb2.at[:, g], xdev[0], b2n[g]) for g in range(4)]
    y1c = [link(sy1.at[d], ry1.at[d], ydev[d]) for d in range(2)]
    y2c = [[link(sy2.at[d, span(h)], ry2.at[d, span(h)], ydev[d], y2n) for h in range(2)] for d in range(2)]
    y2_all = link(sy2, ry2, ydev[0], y2n)
    near = (yp, ym)
    order = (y2, yp, ym, y)

    def unit_cols(i, first, size):
        xt = (x + (2, 1, 3, 0)[i]) % 4
        return pl.ds(pl.multiple_of(xt * 384 + first, 128), size)

    def wide(i):
        m4[i, :, :256] = dot_nn(lk[c], rk[c, :, unit_cols(i, 0, 256)])

    def shared(i):
        right = jnp.concatenate(
            [rk[c, :, unit_cols(i, 256, 128)], rk[c, :, unit_cols(i + 1, 256, 128)]], axis=1
        )
        out = dot_nn(lk[c], right)
        m4[i, :, 256:] = out[:, :128]
        m4[i + 1, :, 256:] = out[:, 128:]

    def first_parts(p):
        cols = slice(parts[p][0], sum(parts[p]))
        for g in range(4):
            for d in range(2):
                sb1[d, g, :, cols] = m4[0, hrow(order[g], 2 + d), cols].astype(BF)
                b1_parts[d][g][p].start()
        for d in range(2):
            sa1[0, d, :, cols] = m4[0, hrow(y2, d), cols].astype(BF)
            a1_parts[d][p].start()

    def a_open(i):
        for d in range(2):
            if i > 0:
                sa1[i, d] = m4[i, hrow(y2, d)].astype(BF)
                a1[i][d].start()
        for d in range(2):
            sa2[i, d, (1 - d) * 48 : (2 - d) * 48] = m4[i, hrow(near[d], 1 - d)].astype(BF)
            a2[i][d][1 - d].start()

    def a_pass(i):
        for d in range(2):
            a1[i][d].wait()
            sa2[i, d, d * 48 : (d + 1) * 48] = (m4[i, hrow(near[d], d)] + ra1[i, d].astype(F32)).astype(BF)
            a2[i][d][d].start()

    def a_final(i):
        a2_all[i].wait()
        ay[i] = m4[i, mrow(y, 0)] + ra2[i, 0].astype(F32) + ra2[i, 1].astype(F32)

    def b_free(d, g):
        free = slice((1 - d) * 48, (2 - d) * 48)
        sb2[d, g, free] = m4[1 + d, hrow(order[g], 3 - d)].astype(BF)
        b2[d][g][1 - d].start()

    def b_pass(d, g):
        held = slice(d * 48, (d + 1) * 48)
        b1[d][g].wait()
        sb2[d, g, held] = (m4[1 + d, hrow(order[g], 2 + d)] + rb1[d, g].astype(F32)).astype(BF)
        b2[d][g][d].start()

    def b_final(g):
        b2_all[g].wait()
        bx[g] = m4[3, mrow(order[g], 1)] + rb2[0, g].astype(F32) + rb2[1, g].astype(F32)

    def open_last(first, value, staged):
        for d in range(2):
            staged[d] = value[0, d * 48 : (d + 1) * 48].astype(BF)
            first[d].start()

    def pass_last(d, first, second, value, staged, got):
        free = slice((1 - d) * 48, (2 - d) * 48)
        held = slice(d * 48, (d + 1) * 48)
        staged[d, free] = value[1 + d, free].astype(BF)
        second[d][1 - d].start()
        first[d].wait()
        staged[d, held] = (value[1 + d, held] + got[d].astype(F32)).astype(BF)
        second[d][d].start()

    wide(0)
    first_parts(0)
    shared(0)
    first_parts(1)
    a_open(0)
    wide(1)
    b_free(0, 0)
    b_free(0, 1)
    a_open(1)
    wide(2)
    b_pass(0, 0)
    b_free(0, 2)
    b_pass(0, 1)
    a_pass(0)
    shared(2)
    b_free(1, 0)
    b_pass(1, 0)
    b_free(1, 1)
    b_pass(1, 1)
    a_open(2)
    b_pass(0, 2)
    b_free(1, 2)
    b_pass(1, 2)
    a_pass(1)
    wide(3)
    a_open(3)
    a_pass(2)
    a_final(0)
    open_last(x1, ay, sx1)
    b_final(0)
    open_last(y1c, bx, sy1)
    a_final(1)
    pass_last(0, x1, x2, ay, sx2, rx1)
    b_free(0, 3)
    b_pass(0, 3)
    a_pass(3)
    b_final(1)
    pass_last(0, y1c, y2c, bx, sy2, ry1)
    a_final(2)
    pass_last(1, x1, x2, ay, sx2, rx1)
    b_free(1, 3)
    b_pass(1, 3)
    b_final(2)
    pass_last(1, y1c, y2c, bx, sy2, ry1)
    a_final(3)

    def third_rows(zz, third):
        base, odd = (zz // 2) * 48, zz % 2
        first = (base + odd * 32, base + 16 + odd * 96, base + 96 + odd * 32)[third]
        return pl.ds(pl.multiple_of(first, 16), 16)

    z_copies = []
    for d in (4, 3, 5, 2, 6, 1, 7):
        zd = (z + d) % 8
        cols = pl.ds(pl.multiple_of((zd % 2) * 128, 128), 256)
        pieces = [
            link(fz.at[third_rows(zd // 2, t), cols], zr.at[d - 1, pl.ds(t * 16, 16)], zdev[d - 1], zn)
            for t in range(3)
        ]
        z_copies.append((zd, pieces))

    def z_send(part):
        for zd, pieces in z_copies:
            pieces[2 * part].start()

            @pl.when((zd // 2) % 2 == part)
            def _():
                pieces[1].start()

    x2_all.wait()
    ft[:96] = ay[3] + rx2[0].astype(F32) + rx2[1].astype(F32)
    fz[:96] = ft[:96].astype(BF)
    z_send(0)
    b_final(3)
    y2_all.wait()
    ft[96:] = bx[3] + ry2[0].astype(F32) + ry2[1].astype(F32)
    fz[96:] = ft[96:].astype(BF)
    z_send(1)
    cols = pl.ds(pl.multiple_of(zl * 128, 128), 256)
    total = jnp.concatenate([ft[third_rows(zh, t), cols] for t in range(3)], axis=0)
    link(zr, zr, zdev[0], zn).wait()
    for d in range(7):
        total = total + zr[d].astype(F32)
    tt[...] = total
    last = link(tt, pt, other)
    last.start()
    gout[c] = total
    last.wait()
    gout[1 - c] = pt[...]

    own_mix.wait()
    all_mix.wait()


def finish(mixed, grads, mixed_out, up_out, down_out):
    gy = lax.axis_index("gy")
    start = (gy // 2) % 2 * 64 + gy % 2 * 96
    mixed_out[...] = mixed[...]
    for i, out in enumerate((up_out, down_out)):
        out[...] = pltpu.roll(grads[i], (256 - start) % 256, 1)[:, :96]


def local(signal, w_up, w_down, cotangent):
    vm = pltpu.VMEM
    dma = pltpu.SemaphoreType.DMA
    anyspec = pl.BlockSpec(memory_space=pl.ANY)
    mixed, grads = pl.pallas_call(
        kernel,
        out_shape=(
            jax.ShapeDtypeStruct((512, D), BF),
            jax.ShapeDtypeStruct((2, 48, 256), F32),
        ),
        in_specs=[anyspec] * 4,
        out_specs=(anyspec, pl.BlockSpec(memory_space=pltpu.VMEM)),
        scratch_shapes=[
            vm((16, CH, D), BF), vm((16, CH, D), BF), vm((ROWS, D2), BF), vm((ROWS, D2), BF),
            vm((4, ROWS, D2), F32), vm((4, ROWS, 1), F32), vm((4, ROWS, FF), F32), vm((ROWS, FF), F32),
            vm((D2, FF), BF), vm((D2, FF), BF), vm((ROWS, D2), F32),
            vm((2, D2, 8 * ROWS), BF), vm((2, 8 * ROWS, FF), BF),
            vm((4, D2, D), F32), vm((4, 96, D), F32), vm((4, 96, D), F32),
            vm((192, D), BF), vm((192, D), F32),
            vm((4, 2, 48, D), BF), vm((4, 2, 48, D), BF),
            vm((4, 2, 96, D), BF), vm((4, 2, 96, D), BF),
            vm((2, 48, D), BF), vm((2, 48, D), BF), vm((2, 96, D), BF), vm((2, 96, D), BF),
            vm((2, 4, 48, D), BF), vm((2, 4, 48, D), BF),
            vm((2, 4, 96, D), BF), vm((2, 4, 96, D), BF),
            vm((2, 48, D), BF), vm((2, 48, D), BF), vm((2, 96, D), BF), vm((2, 96, D), BF),
            vm((7, 48, 256), BF), vm((48, 256), F32), vm((48, 256), F32),
            dma((1,)), dma((1,)), dma((1,)), dma((1,)), dma((1,)), dma((1,)),
            dma((4,)), dma((4,)), dma((4,)), dma((4,)), dma((4,)),
            dma((34,)), dma((34,)),
        ],
        compiler_params=pltpu.CompilerParams(
            collective_id=0, has_side_effects=True, vmem_limit_bytes=62 << 20
        ),
    )(signal, cotangent, w_up, w_down)
    return pl.pallas_call(
        finish,
        out_shape=(
            jax.ShapeDtypeStruct((512, D), BF),
            jax.ShapeDtypeStruct((48, 96), F32),
            jax.ShapeDtypeStruct((48, 96), F32),
        ),
        in_specs=[pl.BlockSpec(memory_space=pltpu.VMEM)] * 2,
        out_specs=(pl.BlockSpec(memory_space=pltpu.VMEM),) * 3,
    )(mixed, grads)


def solution(mesh):
    return jax.shard_map(
        local,
        mesh=mesh,
        in_specs=(P(("gx", "gy"), None), P(), P(), P(("gx", "gy"), None)),
        out_specs=(P(("gx", "gy"), None), P("gx", "gy"), P("gx", "gy")),
        check_vma=False,
    )
```

```python
import math

import jax
import jax.numpy as jnp
from jax import lax
from jax.experimental import pallas as pl
from jax.experimental.pallas import tpu as pltpu
from jax.sharding import PartitionSpec as P

MESH = pl.DeviceIdType.MESH
BF = jnp.bfloat16
F32 = jnp.float32
D = 384
D2 = 768
FF = 1536
CH = 32
ROWS = 256
TILE = 256


def dot_nn(left, right):
    return lax.dot_general(left, right, (((1,), (0,)), ((), ())), preferred_element_type=F32)


def dot_nt(left, right):
    return lax.dot_general(left, right, (((1,), (1,)), ((), ())), preferred_element_type=F32)


def kernel(
    sig, cot, wu_hbm, wd_hbm, mixed, gout,
    xs, gs, nbv, gpv, nf, rs, slope, prev, wu, wd, acc, lk, rk, m4, ay, bx, fz, ft,
    sa1, ra1, sa2, ra2, sx1, rx1, sx2, rx2, sb1, rb1, sb2, rb2, sy1, ry1, sy2, ry2, zr, pt, tt,
    sig_s, sig_r, cot_s, cot_r, mix_s, mix_r, loc, lk_s, lk_r, rk_s, rk_r, red_s, red_r,
):
    gx = lax.axis_index("gx")
    gy = lax.axis_index("gy")
    y, zh = gx // 4, gx % 4
    x, zl, c = gy // 4, (gy // 2) % 2, gy % 2
    z = zh * 2 + zl
    ba, bb, bc = y // 2, zh % 2, x // 2
    me = ba * 8 + bb * 4 + bc * 2 + c

    def at(xx, yy, zz, cc):
        return {"gx": yy * 4 + zz // 2, "gy": xx * 4 + (zz % 2) * 2 + cc}

    yp, ym, y2 = (y + 1) % 4, (y + 3) % 4, (y + 2) % 4
    xp, xm = (x + 1) % 4, (x + 3) % 4
    ydev = (at(x, yp, z, c), at(x, ym, z, c))
    xdev = (at(xp, y, z, c), at(xm, y, z, c))
    zdev = [at(x, y, (z + d) % 8, c) for d in range(1, 8)]
    other = at(x, y, z, 1 - c)
    group = []
    for r in range(1, 16):
        ra, rb, rc, rd = r // 8, (r // 4) % 2, (r // 2) % 2, r % 2
        yy = y + ra * (2 - 4 * ba)
        zz = z + rb * (2 - 4 * bb)
        xx = x + rc * (2 - 4 * bc)
        cc = c + rd * (1 - 2 * c)
        target = (yy // 2) * 8 + ((zz // 2) % 2) * 4 + (xx // 2) * 2 + cc
        group.append((r, at(xx, yy, zz, cc), target))

    load_wu = pltpu.make_async_copy(wu_hbm, wu, loc.at[0])
    load_wd = pltpu.make_async_copy(wd_hbm, wd, loc.at[1])
    load_wu.start()
    load_wd.start()
    own_rows = pl.ds(pl.multiple_of(me * CH, CH), CH)
    own_sig = pltpu.make_async_copy(sig.at[own_rows], xs.at[me], loc.at[2])
    own_cot = pltpu.make_async_copy(cot.at[own_rows], gs.at[me], loc.at[3])
    own_sig.start()
    own_cot.start()

    barrier = pltpu.get_barrier_semaphore()
    peers = [dev for _, dev, _ in group] + zdev + list(ydev) + list(xdev)
    for dev in peers:
        pl.semaphore_signal(barrier, inc=1, device_id=dev, device_id_type=MESH)
    pl.semaphore_wait(barrier, len(peers))

    def remote(src, dst, send, recv, dev):
        return pltpu.make_async_remote_copy(
            src_ref=src, dst_ref=dst, send_sem=send, recv_sem=recv, device_id=dev, device_id_type=MESH
        )

    sig_copies, cot_copies = [], []
    for r, dev, target in reversed(group):
        rows = pl.ds(pl.multiple_of(target * CH, CH), CH)
        sig_copies.append(remote(sig.at[rows], xs.at[me], sig_s.at[0], sig_r.at[0], dev))
        cot_copies.append(remote(cot.at[rows], gs.at[me], cot_s.at[0], cot_r.at[0], dev))
    for copy in sig_copies:
        copy.start()
    load_wu.wait()
    load_wd.wait()
    own_sig.wait()
    most = pl.ds(0, 15)
    wide_rows = pl.ds(0, 15 * CH)
    all_sig = remote(sig.at[wide_rows], xs.at[most], sig_s.at[0], sig_r.at[0], other)
    all_cot = remote(cot.at[wide_rows], gs.at[most], cot_s.at[0], cot_r.at[0], other)
    all_mix = remote(xs.at[most], mixed.at[wide_rows], mix_s.at[0], mix_r.at[0], other)
    all_sig.wait()
    for copy in cot_copies:
        copy.start()

    def low_high(k, i):
        stride = 8 >> k
        low = (i // stride) * 2 * stride + i % stride
        return low, low + stride

    def store_turned(which, t, mine, source):
        turned = source[:, t * TILE : (t + 1) * TILE].T
        for b in range(TILE // 16):
            block = t * (TILE // 16) + b
            group_y, inner = block // 12, block % 12
            zz, third = inner // 3, inner % 3
            odd = zz % 2
            spot = (3 * (zz // 2) + (2 * odd, 1 + 6 * odd, 6 + 2 * odd)[third]) * 16 + group_y * 192
            lk[which, spot : spot + 16, mine] = turned[b * 16 : (b + 1) * 16]

    def send_left(k):
        cols = pl.ds(k * ROWS, ROWS)
        into = pl.ds(4 * ROWS + k * ROWS, ROWS)
        return remote(lk.at[1 - c, :, cols], lk.at[1 - c, :, into], lk_s.at[k], lk_r.at[k], other)

    def send_right(k):
        cols = pl.ds(k * ROWS, ROWS)
        into = pl.ds(4 * ROWS + k * ROWS, ROWS)
        return remote(rk.at[1 - c, cols], rk.at[1 - c, into], rk_s.at[k], rk_r.at[k], other)

    for k in range(4):
        for i in range(8):
            low, high = low_high(k, i)
            rows = pl.ds(i * CH, CH)
            pair = jnp.concatenate([xs[low], xs[high]], axis=1).astype(F32)
            centre = jnp.mean(pair, axis=-1, keepdims=True)
            shifted = pair - centre
            spread = jnp.mean(shifted * shifted, axis=-1, keepdims=True)
            factor = lax.rsqrt(spread + 1e-05)
            normed = shifted * factor
            nf[k, rows] = normed
            rs[k, rows] = factor
            nbv[rows] = normed.astype(BF)
        mine = slice(k * ROWS, (k + 1) * ROWS)
        for j in range(FF // TILE):
            cols = slice(j * TILE, (j + 1) * TILE)
            pre = dot_nn(nbv[...], wu[:, cols])
            half = 0.5 + 0.5 * lax.erf(pre * (1.0 / math.sqrt(2.0)))
            rk[1, mine, cols] = (pre * half).astype(BF)
            prev[:, cols] = pre
            slope[k, :, cols] = half
            if j % 2 == 1:
                store_turned(0, j // 2, mine, nbv)
        for j in range(D2 // TILE):
            cols = slice(j * TILE, (j + 1) * TILE)
            out = dot_nt(rk[1, mine], wd[cols])
            for i in range(8):
                low, high = low_high(k, i)
                for at_pos, first in ((low, 0), (high, D)):
                    lo, hi = max(first, j * TILE), min(first + D, (j + 1) * TILE)
                    if lo < hi:
                        here = slice(lo - first, hi - first)
                        value = out[i * CH : (i + 1) * CH, lo - j * TILE : hi - j * TILE]
                        xs[at_pos, :, here] = (xs[at_pos, :, here].astype(F32) + value).astype(BF)
            for t in (2 * j, 2 * j + 1):
                cols = slice(t * TILE, (t + 1) * TILE)
                pre = prev[:, cols]
                bell = jnp.exp2(pre * pre * (-0.5 * math.log2(math.e)))
                slope[k, :, cols] = slope[k, :, cols] + pre * (1.0 / math.sqrt(2.0 * math.pi)) * bell

        @pl.when(c == 1)
        def _():
            send_left(k).start()

        @pl.when(c == 0)
        def _():
            send_right(k).start()

    mix_copies = []
    for r, dev, target in group:
        mix_copies.append(remote(xs.at[target], mixed.at[own_rows], mix_s.at[0], mix_r.at[0], dev))
    own_mix = pltpu.make_async_copy(xs.at[me], mixed.at[own_rows], loc.at[2])
    own_mix.start()
    for copy in mix_copies:
        copy.start()

    own_cot.wait()
    all_cot.wait()

    for k in (3, 2, 1, 0):
        for i in range(8):
            low, high = low_high(k, i)
            rows = pl.ds(i * CH, CH)
            gpv[rows, :D] = gs[low]
            gpv[rows, D:] = gs[high]
        mine = slice(k * ROWS, (k + 1) * ROWS)
        for j in range(FF // TILE):
            cols = slice(j * TILE, (j + 1) * TILE)
            d_hidden = dot_nn(gpv[...], wd[:, cols])
            rk[0, mine, cols] = (d_hidden * slope[k, :, cols]).astype(BF)
            if j < 3:
                store_turned(1, j, mine, gpv)

        @pl.when(c == 0)
        def _():
            send_left(k).start()

        @pl.when(c == 1)
        def _():
            send_right(k).start()

        if k > 0:
            for j in range(D2 // TILE):
                cols = slice(j * TILE, (j + 1) * TILE)
                acc[:, cols] = dot_nt(rk[0, k * ROWS : (k + 1) * ROWS], wu[cols])
            for i in range(8):
                low, high = low_high(k, i)
                rows = pl.ds(i * CH, CH)
                d_norm = acc[rows]
                normed = nf[k, rows]
                first = jnp.mean(d_norm, axis=-1, keepdims=True)
                second = jnp.mean(d_norm * normed, axis=-1, keepdims=True)
                d_pair = rs[k, rows] * (d_norm - first - normed * second)
                gs[low] = (gs[low].astype(F32) + d_pair[:, :D]).astype(BF)
                gs[high] = (gs[high].astype(F32) + d_pair[:, D:]).astype(BF)

    for k in range(4):
        send_left(k).wait()
        send_right(k).wait()

    count = [0]

    def fresh():
        count[0] += 1
        return count[0] - 1

    def link(src, dst, dev, n=None):
        n = fresh() if n is None else n
        return remote(src, dst, red_s.at[n], red_r.at[n], dev)

    def mrow(group_y, half):
        return pl.ds(pl.multiple_of(group_y * 192 + half * 96, 48), 96)

    def hrow(group_y, part):
        return pl.ds(pl.multiple_of(group_y * 192 + part * 48, 48), 48)

    def span(first, size=48):
        return pl.ds(first * 48, size)

    a1 = [[link(sa1.at[i, d], ra1.at[i, d], ydev[d]) for d in range(2)] for i in range(4)]
    a2n = [fresh() for i in range(4)]
    a2 = [
        [[link(sa2.at[i, d, span(h)], ra2.at[i, d, span(h)], ydev[d], a2n[i]) for h in range(2)] for d in range(2)]
        for i in range(4)
    ]
    a2_all = [link(sa2.at[i], ra2.at[i], ydev[0], a2n[i]) for i in range(4)]
    x1 = [link(sx1.at[d], rx1.at[d], xdev[d]) for d in range(2)]
    x2n, y2n, zn = fresh(), fresh(), fresh()
    x2 = [[link(sx2.at[d, span(h)], rx2.at[d, span(h)], xdev[d], x2n) for h in range(2)] for d in range(2)]
    x2_all = link(sx2, rx2, xdev[0], x2n)
    b1 = [[link(sb1.at[d, g], rb1.at[d, g], xdev[d]) for g in range(4)] for d in range(2)]
    b2n = [fresh() for g in range(4)]
    b2 = [
        [[link(sb2.at[d, g, span(h)], rb2.at[d, g, span(h)], xdev[d], b2n[g]) for h in range(2)] for g in range(4)]
        for d in range(2)
    ]
    b2_all = [link(sb2.at[:, g], rb2.at[:, g], xdev[0], b2n[g]) for g in range(4)]
    y1c = [link(sy1.at[d], ry1.at[d], ydev[d]) for d in range(2)]
    y2c = [[link(sy2.at[d, span(h)], ry2.at[d, span(h)], ydev[d], y2n) for h in range(2)] for d in range(2)]
    y2_all = link(sy2, ry2, ydev[0], y2n)
    near = (yp, ym)
    order = (y2, yp, ym, y)

    def unit_cols(i, first, size):
        xt = (x + (2, 1, 3, 0)[i]) % 4
        return pl.ds(pl.multiple_of(xt * 384 + first, 128), size)

    def wide(i):
        m4[i, :, :256] = dot_nn(lk[c], rk[c, :, unit_cols(i, 0, 256)])

    def shared(i):
        right = jnp.concatenate(
            [rk[c, :, unit_cols(i, 256, 128)], rk[c, :, unit_cols(i + 1, 256, 128)]], axis=1
        )
        out = dot_nn(lk[c], right)
        m4[i, :, 256:] = out[:, :128]
        m4[i + 1, :, 256:] = out[:, 128:]

    def a_open(i):
        for d in range(2):
            sa1[i, d] = m4[i, hrow(y2, d)].astype(BF)
            a1[i][d].start()
        for d in range(2):
            sa2[i, d, (1 - d) * 48 : (2 - d) * 48] = m4[i, hrow(near[d], 1 - d)].astype(BF)
            a2[i][d][1 - d].start()

    def a_pass(i):
        for d in range(2):
            a1[i][d].wait()
            sa2[i, d, d * 48 : (d + 1) * 48] = (m4[i, hrow(near[d], d)] + ra1[i, d].astype(F32)).astype(BF)
            a2[i][d][d].start()

    def a_final(i):
        a2_all[i].wait()
        ay[i] = m4[i, mrow(y, 0)] + ra2[i, 0].astype(F32) + ra2[i, 1].astype(F32)

    def b_open():
        for g in range(4):
            for d in range(2):
                sb1[d, g] = m4[0, hrow(order[g], 2 + d)].astype(BF)
                b1[d][g].start()

    def b_free(d, g):
        free = slice((1 - d) * 48, (2 - d) * 48)
        sb2[d, g, free] = m4[1 + d, hrow(order[g], 3 - d)].astype(BF)
        b2[d][g][1 - d].start()

    def b_pass(d, g):
        held = slice(d * 48, (d + 1) * 48)
        b1[d][g].wait()
        sb2[d, g, held] = (m4[1 + d, hrow(order[g], 2 + d)] + rb1[d, g].astype(F32)).astype(BF)
        b2[d][g][d].start()

    def b_final(g):
        b2_all[g].wait()
        bx[g] = m4[3, mrow(order[g], 1)] + rb2[0, g].astype(F32) + rb2[1, g].astype(F32)

    def open_last(first, value, staged):
        for d in range(2):
            staged[d] = value[0, d * 48 : (d + 1) * 48].astype(BF)
            first[d].start()

    def pass_last(d, first, second, value, staged, got):
        free = slice((1 - d) * 48, (2 - d) * 48)
        held = slice(d * 48, (d + 1) * 48)
        staged[d, free] = value[1 + d, free].astype(BF)
        second[d][1 - d].start()
        first[d].wait()
        staged[d, held] = (value[1 + d, held] + got[d].astype(F32)).astype(BF)
        second[d][d].start()

    wide(0)
    shared(0)
    b_open()
    a_open(0)
    wide(1)
    b_free(0, 0)
    b_free(0, 1)
    a_open(1)
    wide(2)
    b_pass(0, 0)
    b_free(0, 2)
    b_pass(0, 1)
    a_pass(0)
    shared(2)
    b_free(1, 0)
    b_pass(1, 0)
    b_free(1, 1)
    b_pass(1, 1)
    a_open(2)
    b_pass(0, 2)
    b_free(1, 2)
    b_pass(1, 2)
    a_pass(1)
    wide(3)
    a_open(3)
    a_pass(2)
    a_final(0)
    open_last(x1, ay, sx1)
    b_final(0)
    open_last(y1c, bx, sy1)
    a_final(1)
    pass_last(0, x1, x2, ay, sx2, rx1)
    b_free(0, 3)
    b_pass(0, 3)
    a_pass(3)
    b_final(1)
    pass_last(0, y1c, y2c, bx, sy2, ry1)
    a_final(2)
    pass_last(1, x1, x2, ay, sx2, rx1)
    b_free(1, 3)
    b_pass(1, 3)
    b_final(2)
    pass_last(1, y1c, y2c, bx, sy2, ry1)
    a_final(3)

    def third_rows(zz, third):
        base, odd = (zz // 2) * 48, zz % 2
        first = (base + odd * 32, base + 16 + odd * 96, base + 96 + odd * 32)[third]
        return pl.ds(pl.multiple_of(first, 16), 16)

    z_copies = []
    for d in (4, 3, 5, 2, 6, 1, 7):
        zd = (z + d) % 8
        cols = pl.ds(pl.multiple_of((zd % 2) * 128, 128), 256)
        pieces = [
            link(fz.at[third_rows(zd // 2, t), cols], zr.at[d - 1, pl.ds(t * 16, 16)], zdev[d - 1], zn)
            for t in range(3)
        ]
        z_copies.append((zd, pieces))

    def z_send(part):
        for zd, pieces in z_copies:
            pieces[2 * part].start()

            @pl.when((zd // 2) % 2 == part)
            def _():
                pieces[1].start()

    x2_all.wait()
    ft[:96] = ay[3] + rx2[0].astype(F32) + rx2[1].astype(F32)
    fz[:96] = ft[:96].astype(BF)
    z_send(0)
    b_final(3)
    y2_all.wait()
    ft[96:] = bx[3] + ry2[0].astype(F32) + ry2[1].astype(F32)
    fz[96:] = ft[96:].astype(BF)
    z_send(1)
    cols = pl.ds(pl.multiple_of(zl * 128, 128), 256)
    total = jnp.concatenate([ft[third_rows(zh, t), cols] for t in range(3)], axis=0)
    link(zr, zr, zdev[0], zn).wait()
    for d in range(7):
        total = total + zr[d].astype(F32)
    tt[...] = total
    last = link(tt, pt, other)
    last.start()
    gout[c] = total
    last.wait()
    gout[1 - c] = pt[...]

    own_mix.wait()
    all_mix.wait()


def finish(mixed, grads, mixed_out, up_out, down_out):
    gy = lax.axis_index("gy")
    start = (gy // 2) % 2 * 64 + gy % 2 * 96
    mixed_out[...] = mixed[...]
    for i, out in enumerate((up_out, down_out)):
        out[...] = pltpu.roll(grads[i], (256 - start) % 256, 1)[:, :96]


def local(signal, w_up, w_down, cotangent):
    vm = pltpu.VMEM
    dma = pltpu.SemaphoreType.DMA
    anyspec = pl.BlockSpec(memory_space=pl.ANY)
    mixed, grads = pl.pallas_call(
        kernel,
        out_shape=(
            jax.ShapeDtypeStruct((512, D), BF),
            jax.ShapeDtypeStruct((2, 48, 256), F32),
        ),
        in_specs=[anyspec] * 4,
        out_specs=(anyspec, pl.BlockSpec(memory_space=pltpu.VMEM)),
        scratch_shapes=[
            vm((16, CH, D), BF), vm((16, CH, D), BF), vm((ROWS, D2), BF), vm((ROWS, D2), BF),
            vm((4, ROWS, D2), F32), vm((4, ROWS, 1), F32), vm((4, ROWS, FF), F32), vm((ROWS, FF), F32),
            vm((D2, FF), BF), vm((D2, FF), BF), vm((ROWS, D2), F32),
            vm((2, D2, 8 * ROWS), BF), vm((2, 8 * ROWS, FF), BF),
            vm((4, D2, D), F32), vm((4, 96, D), F32), vm((4, 96, D), F32),
            vm((192, D), BF), vm((192, D), F32),
            vm((4, 2, 48, D), BF), vm((4, 2, 48, D), BF),
            vm((4, 2, 96, D), BF), vm((4, 2, 96, D), BF),
            vm((2, 48, D), BF), vm((2, 48, D), BF), vm((2, 96, D), BF), vm((2, 96, D), BF),
            vm((2, 4, 48, D), BF), vm((2, 4, 48, D), BF),
            vm((2, 4, 96, D), BF), vm((2, 4, 96, D), BF),
            vm((2, 48, D), BF), vm((2, 48, D), BF), vm((2, 96, D), BF), vm((2, 96, D), BF),
            vm((7, 48, 256), BF), vm((48, 256), F32), vm((48, 256), F32),
            dma((1,)), dma((1,)), dma((1,)), dma((1,)), dma((1,)), dma((1,)),
            dma((4,)), dma((4,)), dma((4,)), dma((4,)), dma((4,)),
            dma((32,)), dma((32,)),
        ],
        compiler_params=pltpu.CompilerParams(
            collective_id=0, has_side_effects=True, vmem_limit_bytes=62 << 20
        ),
    )(signal, cotangent, w_up, w_down)
    return pl.pallas_call(
        finish,
        out_shape=(
            jax.ShapeDtypeStruct((512, D), BF),
            jax.ShapeDtypeStruct((48, 96), F32),
            jax.ShapeDtypeStruct((48, 96), F32),
        ),
        in_specs=[pl.BlockSpec(memory_space=pltpu.VMEM)] * 2,
        out_specs=(pl.BlockSpec(memory_space=pltpu.VMEM),) * 3,
    )(mixed, grads)


def solution(mesh):
    return jax.shard_map(
        local,
        mesh=mesh,
        in_specs=(P(("gx", "gy"), None), P(), P(), P(("gx", "gy"), None)),
        out_specs=(P(("gx", "gy"), None), P("gx", "gy"), P("gx", "gy")),
        check_vma=False,
    )
```
